128 devices in a mesh: blk: 8 (over x, y_lo), dom: 16 (over z, y_hi, core).
Axes of the slice: x: 4, y: 4 (y_hi: 2, y_lo: 2; y = y_hi * 2 + y_lo), z: 4, core: 2. Of those that a mesh axis runs over, the one named last changes fastest.
Arguments:
- positions: float32 [3, 131072], P(None, ('blk', 'dom')), may hold values from -6 to 6
- line_vectors: float32 [3, 131072], P(None, ('blk', 'dom')), may hold values from -6 to 6
- burgers: float32 [3, 131072], P(None, ('blk', 'dom')), may hold values from -6 to 6
- mobility: float32 [131072], P(('blk', 'dom')), may hold values from 0.5 to 2
- close_list: int32 [32, 131072], P(None, ('blk', 'dom')), may hold values from 0 to 256, as said below
- ghost_map: int32 [4, 65536], P(None, ('blk', 'dom')), may hold values from 0 to 1023, as said below
Outputs:
- new_positions: float32 [3, 131072], P(None, ('blk', 'dom'))
- velocity: float32 [3, 131072], P(None, ('blk', 'dom'))
The draws below stay inside these ranges and needn't reach their ends.
Inputs may be any that keep to these rules, and one draw needn't show every extreme that they name: `close_list`: each entry is a place in the window of the segment's cell: below 128 a segment of the same cell, 128 + u the u-th row of the cell's ghost window, and 256 an empty slot. `ghost_map`: for each subcycle, each device's run of 512 entries holds first 256 distinct local segment numbers below 512 (the ghosts of the lower domain), the first of them 0, then 256 distinct local numbers of at least 1024 - 512 (the ghosts of the upper domain), the first of them 1024 - 1.
All inputs are finite; a program needn't handle non-finite values.
Results may differ from the reference program's by a relative error of at most 0.0005.
Values sent between devices are 32-bit elements; how exact they have to be, the bound alone decides.
A program may use at most 64 MiB of HBM per device.

```python
import math
import jax
import jax.numpy as jnp
from jax import lax

CELLS = 8
CELL_SEGS = 128
SLOTS = 32
GHOSTS = 256
SUBS = 4
SEG_DEV = 1024
RIM_ROWS = 512
WINDOWS = 4
SEGS = 131072
N_BLK = 8
N_DOM = 16


def draw_close_list(key, part):
    device_count = SEGS // SEG_DEV
    empty_slot = 2 * CELL_SEGS
    fill_key, level_key, index_key = jax.random.split(key, 3)
    levels = jax.random.randint(level_key, (device_count,), 3, 10)
    level_rows = jnp.repeat(levels, SEG_DEV)
    chance = jax.random.randint(fill_key, (SLOTS, SEGS), 0, 10)
    partner = jax.random.randint(index_key, (SLOTS, SEGS), 0, empty_slot)
    return jnp.where(chance < level_rows[None, :], partner, empty_slot).astype(jnp.int32)


def draw_ghost_map(key, part):
    device_count = SEGS // SEG_DEV
    key_list = jax.random.split(key, SUBS * device_count * 2)

    def one_side(one_key):
        picked = jax.random.permutation(one_key, RIM_ROWS - 1)[:GHOSTS - 1] + 1
        return jnp.concatenate([jnp.zeros((1,), jnp.int32), picked.astype(jnp.int32)])
    side_rows = jax.vmap(one_side)(key_list).reshape(SUBS, device_count, 2, GHOSTS)
    lower_side = side_rows[:, :, 0]
    upper_side = SEG_DEV - 1 - side_rows[:, :, 1]
    return jnp.stack([lower_side, upper_side], 2).reshape(SUBS, device_count * 2 * GHOSTS).astype(jnp.int32)


def level_of(key, dims, cuts, least, largest):
    gain, own = 1.0, jax.random.fold_in(key, 6)
    for axis_at, shards_of in cuts:
        steps = jnp.exp(jax.random.uniform(jax.random.fold_in(own, axis_at), (shards_of,), jnp.float32, least / len(cuts), largest / len(cuts)))
        gain = gain * jnp.repeat(steps, dims[axis_at] // shards_of).reshape([-1 if axis == axis_at else 1 for axis in range(len(dims))])
    return gain


def centred(key, extent, spread, limit, cuts=(), kind=jnp.bfloat16):
    factor_of = level_of(key, extent, cuts, -0.22, 0.18) if cuts else 1.0
    array = jax.random.normal(key, extent, jnp.float32) * spread * factor_of
    return jnp.minimum(jnp.maximum(array, -limit), limit).astype(kind)


def setup_inputs(seed: int = 0) -> dict:
    key_of = jax.random.split(jax.random.key(seed), 7)
    return {
        "positions": centred(key_of[0], (3, SEGS), 1.0, 6.0, ((1, 128),), jnp.float32),
        "line_vectors": centred(key_of[1], (3, SEGS), 1.0, 6.0, ((1, 128),), jnp.float32),
        "burgers": centred(key_of[2], (3, SEGS), 1.0, 6.0, ((1, 128),), jnp.float32),
        "mobility": jnp.clip(jnp.exp(math.log(2.0) - 1.3862944 * jax.random.uniform(key_of[3], (SEGS,), jnp.float32) ** level_of(key_of[3], (SEGS,), ((0, 128),), -0.2, 0.2)), 0.5, 2.0),
        "close_list": draw_close_list(jax.random.fold_in(key_of[6], 71), 0),
        "ghost_map": draw_ghost_map(jax.random.fold_in(key_of[6], 71), 0),
    }


long_core = 1.0
short_core = 0.25
time_step = 0.05

def pair_weights(target, source, core):
    delta_x = target[0][..., :, None] - source[0][..., None, :]
    delta_y = target[1][..., :, None] - source[1][..., None, :]
    delta_z = target[2][..., :, None] - source[2][..., None, :]
    radius = delta_x * delta_x + delta_y * delta_y + delta_z * delta_z + core * core
    inverse = lax.rsqrt(radius)
    line_dot = target[3][..., :, None] * source[3][..., None, :] + target[4][..., :, None] * source[4][..., None, :] + target[5][..., :, None] * source[5][..., None, :]
    burgers_dot = target[6][..., :, None] * source[6][..., None, :] + target[7][..., :, None] * source[7][..., None, :] + target[8][..., :, None] * source[8][..., None, :]
    weight = burgers_dot * line_dot * inverse * inverse * inverse
    return (weight, (delta_x, delta_y, delta_z))

def cell_force(target, source):
    weight, deltas = pair_weights(target, source, long_core)
    return jnp.stack([lax.optimization_barrier(jnp.sum(weight * delta, axis=-1)) for delta in deltas])

def slot_force(own_rows, partners):
    delta_x = own_rows[0][None] - partners[0]
    delta_y = own_rows[1][None] - partners[1]
    delta_z = own_rows[2][None] - partners[2]
    radius = delta_x * delta_x + delta_y * delta_y + delta_z * delta_z + short_core * short_core
    inverse = lax.rsqrt(radius)
    line_dot = own_rows[3][None] * partners[3] + own_rows[4][None] * partners[4] + own_rows[5][None] * partners[5]
    burgers_dot = own_rows[6][None] * partners[6] + own_rows[7][None] * partners[7] + own_rows[8][None] * partners[8]
    weight = burgers_dot * line_dot * inverse * inverse * inverse
    return jnp.stack([lax.optimization_barrier(jnp.sum(weight * delta_x, 0)), lax.optimization_barrier(jnp.sum(weight * delta_y, 0)), lax.optimization_barrier(jnp.sum(weight * delta_z, 0))])

def long_range(seg_state):
    cycle_reach = N_BLK // 4
    device_count = N_BLK * N_DOM
    cell_rows = seg_state.reshape(9, device_count, CELLS, CELL_SEGS)

    def per_device(device):
        block_id = device // N_DOM
        domain = device % N_DOM
        target = jnp.take(cell_rows, device, axis=1)
        summed = cell_force(target, target)
        for offset in range(1, cycle_reach + 1):
            for direction in (1, -1):
                source_dev = (block_id + direction * offset + N_BLK) % N_BLK * N_DOM + domain
                summed = summed + cell_force(target, jnp.take(cell_rows, source_dev, axis=1))
        return summed.reshape(3, -1)
    forces = lax.map(per_device, jnp.arange(device_count, dtype=jnp.int32))
    return jnp.moveaxis(forces, 0, 1).reshape(3, -1) / math.sqrt((2 * cycle_reach + 1) * CELL_SEGS)

def window_places(close_rows):
    seg_index = jnp.arange(SEG_DEV, dtype=jnp.int32)
    cell_index = seg_index // CELL_SEGS
    own_place = cell_index[None, :] * CELL_SEGS + close_rows
    ghost_place = SEG_DEV + cell_index[None, :] % WINDOWS * CELL_SEGS + (close_rows - CELL_SEGS)
    empty_place = SEG_DEV + 2 * GHOSTS
    places = jnp.where(close_rows < CELL_SEGS, own_place, jnp.where(close_rows < 2 * CELL_SEGS, ghost_place, empty_place))
    return places.astype(jnp.int32)

def short_range(current, statics, close_list, map_rows):
    device_count = N_BLK * N_DOM
    full_rows = jnp.concatenate([current, statics], 0).reshape(9, device_count, -1)
    close_rows = close_list.reshape(SLOTS, device_count, -1)

    def per_device(device):
        block_id = device // N_DOM
        domain = device % N_DOM
        lower_dev = block_id * N_DOM + (domain + N_DOM - 1) % N_DOM
        upper_dev = block_id * N_DOM + (domain + 1) % N_DOM
        own_rows = jnp.take(full_rows, device, axis=1)
        from_lower = jnp.take(jnp.take(full_rows, lower_dev, axis=1), jnp.take(map_rows, lower_dev, axis=0)[GHOSTS:], axis=1)
        from_upper = jnp.take(jnp.take(full_rows, upper_dev, axis=1), jnp.take(map_rows, upper_dev, axis=0)[:GHOSTS], axis=1)
        extended_rows = jnp.concatenate([own_rows, from_lower, from_upper], 1)
        places = window_places(jnp.take(close_rows, device, axis=1))
        partners = jnp.take(extended_rows, places, axis=1, mode='fill', fill_value=0.0)
        return slot_force(own_rows, partners)
    forces = lax.map(per_device, jnp.arange(device_count, dtype=jnp.int32))
    return jnp.moveaxis(forces, 0, 1).reshape(3, -1) / math.sqrt(SLOTS)

def reference(positions, line_vectors, burgers, mobility, close_list, ghost_map):
    statics = jnp.concatenate([line_vectors, burgers], 0)
    long_force = long_range(jnp.concatenate([positions, statics], 0))
    velocity = jnp.zeros_like(positions)
    for subcycle in range(SUBS):
        map_rows = ghost_map[subcycle].reshape(N_BLK * N_DOM, 2 * GHOSTS)
        first_vel = mobility * (long_force + short_range(positions, statics, close_list, map_rows))
        guess_pos = positions + time_step * first_vel
        second = mobility * (long_force + short_range(guess_pos, statics, close_list, map_rows))
        velocity = 0.5 * (first_vel + second)
        positions = positions + time_step * velocity
    return (positions, velocity)
```

```python
import functools
import math

import jax
import jax.numpy as jnp
from jax import lax
from jax.experimental import pallas as pl
from jax.experimental.pallas import tpu as pltpu
from jax.sharding import PartitionSpec as P

MESH = pl.DeviceIdType.MESH
F32 = jnp.float32
BF16 = jnp.bfloat16

LANES = 128
SLOTS = 32
SUBS = 4
LONG_CORE = 1.0
SHORT_CORE = 0.25
STEP = 0.05

ROWS_X = 24
ROWS_XLB = 72
ROWS_SETUP = 80
ROW_MOB = 72
ROW_F = 80
ROWS_ALL = 112


def take_lanes(rows, lane):
    return jnp.take_along_axis(rows, lane, axis=1, mode="promise_in_bounds")


def split3(value):
    high = value.astype(BF16)
    rest = value - high.astype(F32)
    mid = rest.astype(BF16)
    low = (rest - mid.astype(F32)).astype(BF16)
    return high.astype(F32), mid.astype(F32), low.astype(F32)


def kernel(
    n_blk,
    n_dom,
    pos_hbm,
    lin_hbm,
    bur_hbm,
    mob_hbm,
    clo_hbm,
    map_hbm,
    new_ref,
    vel_ref,
    pos_v,
    lin_v,
    bur_v,
    mob_v,
    state,
    far_blk,
    dom_in,
    force_in,
    merged,
    close,
    maps,
    map_all,
    feat,
    lhs,
    acc,
    statics_gh,
    weight_own,
    weight,
    ghost,
    frow,
    guess,
    xsend,
    xrecv,
    xx,
    local_sem,
    send_sem,
    recv_sem,
):
    me_b = lax.axis_index("blk")
    me_d = lax.axis_index("dom")

    def peer(db, dd):
        return {
            "blk": lax.rem(me_b + db + n_blk, n_blk),
            "dom": lax.rem(me_d + dd + n_dom, n_dom),
        }

    blk_steps = (1, -1, 2, -2)
    dom_steps = (-1, 1, -2, 2)

    local = []
    for i, (src, dst) in enumerate(
        (
            (pos_hbm, pos_v),
            (lin_hbm, lin_v),
            (bur_hbm, bur_v),
            (mob_hbm, mob_v),
            (clo_hbm, close.at[:, pl.ds(0, 1024)]),
            (map_hbm, maps.at[0]),
        )
    ):
        copy = pltpu.make_async_copy(src, dst, local_sem.at[i])
        copy.start()
        local.append(copy)

    barrier = pltpu.get_barrier_semaphore()
    for step in blk_steps:
        pl.semaphore_signal(barrier, inc=1, device_id=peer(step, 0), device_id_type=MESH)
    for step in dom_steps:
        pl.semaphore_signal(barrier, inc=1, device_id=peer(0, step), device_id_type=MESH)

    for copy in local[:4]:
        copy.wait()
    for first, ref in ((0, pos_v), (24, lin_v), (48, bur_v), (72, mob_v)):
        for k in range(ref.shape[0]):
            for q in range(8):
                state[pl.ds(first + k * 8 + q, 1), :] = ref[pl.ds(k, 1), pl.ds(q * LANES, LANES)]

    pl.semaphore_wait(barrier, 8)

    sends = []

    def send(src, dst, device):
        i = len(sends)
        copy = pltpu.make_async_remote_copy(
            src_ref=src,
            dst_ref=dst,
            send_sem=send_sem.at[i],
            recv_sem=recv_sem.at[i],
            device_id=device,
            device_id_type=MESH,
        )
        copy.start()
        sends.append(copy)
        return copy

    blk_copies = [
        send(state.at[pl.ds(0, ROWS_XLB)], far_blk.at[i], peer(step, 0))
        for i, step in enumerate(blk_steps)
    ]
    dom_copies = [
        send(
            state.at[pl.ds(0, ROWS_SETUP)],
            dom_in.at[i, pl.ds(0, ROWS_SETUP)],
            peer(0, step),
        )
        for i, step in enumerate(dom_steps)
    ]
    dom_copies += [
        send(map_hbm, maps.at[1 + i], peer(0, step)) for i, step in enumerate(dom_steps)
    ]
    dom_copies += [
        send(
            clo_hbm.at[:, pl.ds(i * 512, 512)],
            close.at[:, pl.ds(1024 + i * 512, 512)],
            peer(0, step),
        )
        for i, step in enumerate(dom_steps[:2])
    ]

    def centre(rows):
        return jnp.mean(rows, axis=1, keepdims=True)

    own_pos = [state[pl.ds(8 * k, 8), :] for k in range(3)]
    centres = [centre(rows) for rows in own_pos]
    one = jnp.ones((8, LANES), F32)
    zero = jnp.zeros((8, LANES), F32)

    def features(rows_of, target):
        pos = [rows_of(k) - centres[k] for k in range(3)]
        line = [rows_of(3 + k) for k in range(3)]
        burg = [rows_of(6 + k) for k in range(3)]
        square = pos[0] * pos[0] + pos[1] * pos[1] + pos[2] * pos[2]
        products = [b * l for b in burg for l in line]
        if target:
            rest = [-2.0 * p for p in pos] + [square, one, zero, zero]
        else:
            rest = pos + [one, square + LONG_CORE * LONG_CORE, zero, zero]
        return products + rest

    for f, value in enumerate(features(lambda k: state[pl.ds(8 * k, 8), :], True)):
        for piece, part in enumerate(split3(value)):
            feat[0, pl.ds((piece * 16 + f) * 8, 8), :] = part
    row16 = lax.broadcasted_iota(jnp.int32, (16, LANES), 0)
    numerator_row = row16 < 9

    def build(q, carry):
        part = [feat[0, pl.ds(piece * 128 + q, 16, stride=8), :] for piece in range(3)]
        order = (0, 0, 1, 0, 1, 2)
        for half in range(2):
            keep = numerator_row if half == 0 else jnp.logical_not(numerator_row)
            rows = jnp.concatenate(
                [jnp.where(keep, part[i], 0.0) for i in order]
                + [jnp.zeros((32, LANES), F32)],
                axis=0,
            )
            lhs[q, pl.ds(half * LANES, LANES), :] = rows.T.astype(BF16)
        return carry

    lax.fori_loop(0, 8, build, 0)

    def long_block(source_rows, s):
        for f, value in enumerate(features(source_rows, False)):
            for piece, part in enumerate(split3(value)):
                feat[0, pl.ds((piece * 16 + f) * 8, 8), :] = part
        for k in range(3):
            feat[1, pl.ds(8 * k, 8), :] = source_rows(k) - centres[k]

        def cell(q, carry):
            part = [feat[0, pl.ds(piece * 128 + q, 16, stride=8), :] for piece in range(3)]
            order = (0, 1, 0, 2, 1, 0)
            rhs = jnp.concatenate(
                [part[i] for i in order] + [jnp.zeros((32, LANES), F32)], axis=0
            ).astype(BF16)
            both = jnp.dot(lhs[q], rhs, preferred_element_type=F32)
            inverse = lax.rsqrt(both[LANES:])
            w = both[:LANES] * inverse * (inverse * inverse)
            for k in range(4):
                term = w if k == 3 else w * feat[1, pl.ds(8 * k + q, 1), :]
                if s == 0:
                    acc[q, k] = term
                else:
                    acc[q, k] += term
            return carry

        lax.fori_loop(0, 8, cell, 0)

    long_block(lambda k: state[pl.ds(8 * k, 8), :], 0)
    for i in range(4):
        blk_copies[i].wait_recv()
        long_block(lambda k: far_blk[i, pl.ds(8 * k, 8), :], i + 1)

    cell8 = lax.broadcasted_iota(jnp.int32, (8, LANES), 0)

    def reduce_cell(q, sums):
        pick = jnp.where(cell8 == q, 1.0, 0.0)
        return tuple(
            total
            + lax.dot_general(
                pick,
                acc[q, k],
                (((1,), (1,)), ((), ())),
                precision=lax.Precision.HIGHEST,
                preferred_element_type=F32,
            )
            for k, total in enumerate(sums)
        )

    sums = lax.fori_loop(0, 8, reduce_cell, (zero,) * 4)
    scale = 1.0 / math.sqrt(5 * LANES)
    for k in range(3):
        force = ((own_pos[k] - centres[k]) * sums[3] - sums[k]) * scale
        state[pl.ds(ROW_F + 8 * k, 8), :] = force
    force_copies = [
        send(state.at[pl.ds(ROW_F, 24)], force_in.at[i], peer(0, step))
        for i, step in enumerate(dom_steps[:2])
    ]

    for copy in local[4:]:
        copy.wait()
    for copy in dom_copies:
        copy.wait_recv()
    low_half = cell8 < 4
    for slot in range(5):
        for j in range(4):
            map_all[pl.ds((slot * 4 + j) * SUBS, SUBS), :] = maps[slot, :, pl.ds(j * LANES, LANES)]
    for k in range(10):
        rows = pl.ds(8 * k, 8)
        merged[0, rows, :] = jnp.where(low_half, dom_in[0, rows, :], dom_in[1, rows, :])
        merged[1, rows, :] = jnp.where(low_half, dom_in[2, rows, :], dom_in[3, rows, :])

    windows = []
    for slot_low, buf_low, slot_high, buf_high in ((2, 1, 1, 1), (0, 0, 3, 2), (4, 2, 0, 0)):
        for w in range(4):
            if w < 2:
                windows.append((buf_low, 4, slot_low, 256 + w * LANES))
            else:
                windows.append((buf_high, 0, slot_high, (w - 2) * LANES))

    def pick_window(tiles, index):
        lane = index & 127
        tile = (index >> 7) & 3
        rows = [take_lanes(t, lane) for t in tiles]
        low = jnp.where((tile & 1) == 0, rows[0], rows[1])
        high = jnp.where((tile & 1) == 0, rows[2], rows[3])
        return jnp.where(tile < 2, low, high)

    def map_rows(t, window):
        _, _, slot, first = window
        row = (slot * 4 + first // LANES) * SUBS + t
        return jnp.broadcast_to(map_all[pl.ds(row, 1), :], (8, LANES))

    def static_tile(buf, s):
        if buf == 0:
            return state[pl.ds(24 + s, 8, stride=8), :]
        return merged[buf - 1, pl.ds(24 + s, 8, stride=8), :]

    def own_row(e, k):
        return xx[pl.ds(k * 16 + e, 1), :]

    for k in range(6):
        xx[pl.ds(k * 16, 8), :] = state[pl.ds(24 + 8 * k, 8), :]
        xx[pl.ds(k * 16 + 8, 8), :] = merged[0, pl.ds(24 + 8 * k, 8), :]

    def dots(e, partner):
        line = (
            own_row(e, 0) * partner(0) + own_row(e, 1) * partner(1) + own_row(e, 2) * partner(2)
        )
        burg = (
            own_row(e, 3) * partner(3) + own_row(e, 4) * partner(4) + own_row(e, 5) * partner(5)
        )
        return line * burg

    def close_of(e):
        return close[:, pl.ds(pl.multiple_of(e * LANES, LANES), LANES)]

    def weights_own(e, carry):
        index = close_of(e)
        lane = index & 127

        def partner(k):
            return take_lanes(jnp.broadcast_to(own_row(e, k), (SLOTS, LANES)), lane)

        weight_own[e] = jnp.where(index < LANES, dots(e, partner), 0.0)
        return carry

    lax.fori_loop(0, 16, weights_own, 0)

    def window_of(e):
        return jnp.where(e < 8, lax.rem(e, 4), e - 4)

    def weights_ghost(t, carry):
        for w, window in enumerate(windows):
            buf, first, _, _ = window
            tiles = [static_tile(buf, first + i) for i in range(4)]
            statics_gh[pl.ds(w * 8, 8), :] = pick_window(tiles, map_rows(t, window))

        def one(e, carry):
            index = close_of(e)
            lane = index & 127
            base = window_of(e) * 8

            def partner(k):
                row = statics_gh[pl.ds(base + k, 1), :]
                return take_lanes(jnp.broadcast_to(row, (SLOTS, LANES)), lane)

            value = jnp.where(
                index < LANES,
                weight_own[e],
                jnp.where(index < 2 * LANES, dots(e, partner), 0.0),
            )
            weight[t, e] = value
            return carry

        lax.fori_loop(0, 16, one, 0)
        return carry

    lax.fori_loop(0, SUBS, weights_ghost, 0)

    def fill_ghosts(t, tile_of, count):
        for w, window in enumerate(windows[:count]):
            buf, first, _, _ = window
            tiles = [tile_of(buf, first + i) for i in range(4)]
            ghost[pl.ds(w * 8, 8), :] = pick_window(tiles, map_rows(t, window))

    def evaluate(t, rows, count):
        def one(e, carry):
            index = close_of(e)
            lane = index & 127
            is_ghost = (index & 128) != 0
            base = window_of(e) * 8
            deltas = []
            for k in range(3):
                own = rows[pl.ds(k * 16 + e, 1), :]
                other = ghost[pl.ds(base + k, 1), :]
                picked = jnp.where(
                    is_ghost,
                    take_lanes(jnp.broadcast_to(other, (SLOTS, LANES)), lane),
                    take_lanes(jnp.broadcast_to(own, (SLOTS, LANES)), lane),
                )
                deltas.append(own - picked)
            radius = (
                deltas[0] * deltas[0]
                + deltas[1] * deltas[1]
                + deltas[2] * deltas[2]
                + SHORT_CORE * SHORT_CORE
            )
            inverse = lax.rsqrt(radius)
            w = weight[t, e] * inverse * (inverse * inverse)
            for k in range(3):
                frow[pl.ds(k * 16 + e, 1), :] = jnp.sum(w * deltas[k], axis=0, keepdims=True)
            return carry

        lax.fori_loop(0, count, one, 0)

    short_scale = 1.0 / math.sqrt(SLOTS)
    mob_own = state[pl.ds(ROW_MOB, 8), :]
    mob_rim = merged[0, pl.ds(ROW_MOB, 8), :]

    for copy in force_copies:
        copy.wait_recv()
    for k in range(3):
        rows = pl.ds(8 * k, 8)
        merged[0, pl.ds(ROW_F + 8 * k, 8), :] = jnp.where(
            low_half, force_in[0, rows, :], force_in[1, rows, :]
        )

    for k in range(3):
        xx[pl.ds(k * 16, 8), :] = state[pl.ds(8 * k, 8), :]
        xx[pl.ds(k * 16 + 8, 8), :] = merged[0, pl.ds(8 * k, 8), :]
        guess[pl.ds(128 + k * 8, 8), :] = merged[1, pl.ds(8 * k, 8), :]

    def tile_now(buf, s):
        if buf == 2:
            return guess[pl.ds(128 + s, 8, stride=8), :]
        return xx[pl.ds(buf * 8 + s, 8, stride=16), :]

    def tile_guess(buf, s):
        return guess[pl.ds(buf * 8 + s, 8, stride=16), :]

    for t in range(SUBS):
        fill_ghosts(t, tile_now, 12)
        evaluate(t, xx, 16)
        firsts = []
        for k in range(3):
            for half, mob in ((0, mob_own), (1, mob_rim)):
                long_force = (
                    state[pl.ds(ROW_F + 8 * k, 8), :]
                    if half == 0
                    else merged[0, pl.ds(ROW_F + 8 * k, 8), :]
                )
                rows = pl.ds(k * 16 + half * 8, 8)
                first = mob * (long_force + frow[rows, :] * short_scale)
                guess[rows, :] = xx[rows, :] + STEP * first
                if half == 0:
                    firsts.append(first)
        fill_ghosts(t, tile_guess, 4)
        evaluate(t, guess, 8)
        for k in range(3):
            rows = pl.ds(k * 16, 8)
            second = mob_own * (
                state[pl.ds(ROW_F + 8 * k, 8), :] + frow[rows, :] * short_scale
            )
            velocity = 0.5 * (firsts[k] + second)
            position = xx[rows, :] + STEP * velocity
            if t < SUBS - 1:
                xsend[t, pl.ds(8 * k, 8), :] = position
                xx[rows, :] = position
            else:
                for q in range(8):
                    cols = pl.ds(q * LANES, LANES)
                    new_ref[pl.ds(k, 1), cols] = position[q : q + 1, :]
                    vel_ref[pl.ds(k, 1), cols] = velocity[q : q + 1, :]
        if t < SUBS - 1:
            copies = [
                send(xsend.at[t], xrecv.at[t, i], peer(0, step))
                for i, step in enumerate(dom_steps)
            ]
            for copy in copies:
                copy.wait_recv()
            for k in range(3):
                rows = pl.ds(8 * k, 8)
                xx[pl.ds(k * 16 + 8, 8), :] = jnp.where(
                    low_half, xrecv[t, 0, rows, :], xrecv[t, 1, rows, :]
                )
                guess[pl.ds(128 + k * 8, 8), :] = jnp.where(
                    low_half, xrecv[t, 2, rows, :], xrecv[t, 3, rows, :]
                )

    for copy in sends:
        copy.wait_send()


def solution(mesh):
    n_blk, n_dom = mesh.shape["blk"], mesh.shape["dom"]

    def step(positions, line_vectors, burgers, mobility, close_list, ghost_map):
        count = positions.shape[1]
        anywhere = pl.BlockSpec(memory_space=pl.ANY)
        vmem = pl.BlockSpec(memory_space=pltpu.VMEM)
        shape = jax.ShapeDtypeStruct((3, count), F32)
        n_sends = 4 + 4 + 4 + 2 + 2 + 4 * (SUBS - 1)
        return pl.pallas_call(
            functools.partial(kernel, n_blk, n_dom),
            out_shape=(shape, shape),
            in_specs=[anywhere] * 6,
            out_specs=(vmem, vmem),
            scratch_shapes=[
                pltpu.VMEM((3, count), F32),
                pltpu.VMEM((3, count), F32),
                pltpu.VMEM((3, count), F32),
                pltpu.VMEM((1, count), F32),
                pltpu.VMEM((ROWS_ALL, LANES), F32),
                pltpu.VMEM((4, ROWS_XLB, LANES), F32),
                pltpu.VMEM((4, ROWS_SETUP, LANES), F32),
                pltpu.VMEM((2, 24, LANES), F32),
                pltpu.VMEM((2, ROWS_ALL, LANES), F32),
                pltpu.VMEM((SLOTS, 2 * count), jnp.int32),
                pltpu.VMEM((5, SUBS, 512), jnp.int32),
                pltpu.VMEM((80, LANES), jnp.int32),
                pltpu.VMEM((2, 384, LANES), F32),
                pltpu.VMEM((8, 256, LANES), BF16),
                pltpu.VMEM((8, 4, LANES, LANES), F32),
                pltpu.VMEM((96, LANES), F32),
                pltpu.VMEM((16, SLOTS, LANES), F32),
                pltpu.VMEM((SUBS, 16, SLOTS, LANES), F32),
                pltpu.VMEM((96, LANES), F32),
                pltpu.VMEM((48, LANES), F32),
                pltpu.VMEM((192, LANES), F32),
                pltpu.VMEM((SUBS, 24, LANES), F32),
                pltpu.VMEM((SUBS, 4, 24, LANES), F32),
                pltpu.VMEM((128, LANES), F32),
                pltpu.SemaphoreType.DMA((6,)),
                pltpu.SemaphoreType.DMA((n_sends,)),
                pltpu.SemaphoreType.DMA((n_sends,)),
            ],
            compiler_params=pltpu.CompilerParams(collective_id=0, has_side_effects=True),
        )(positions, line_vectors, burgers, mobility.reshape(1, count), close_list, ghost_map)

    both = ("blk", "dom")
    return jax.shard_map(
        step,
        mesh=mesh,
        in_specs=(
            P(None, both),
            P(None, both),
            P(None, both),
            P(both),
            P(None, both),
            P(None, both),
        ),
        out_specs=(P(None, both), P(None, both)),
        check_vma=False,
    )
```

```python
import functools
import math

import jax
import jax.numpy as jnp
from jax import lax
from jax.experimental import pallas as pl
from jax.experimental.pallas import tpu as pltpu
from jax.sharding import PartitionSpec as P

MESH = pl.DeviceIdType.MESH
F32 = jnp.float32
BF16 = jnp.bfloat16

LANES = 128
CELLS = 8
SLOTS = 32
SUBS = 4
LONG_CORE = 1.0
SHORT_CORE = 0.25
STEP = 0.05

ROWS_SETUP = 80
ROW_MOB = 72
ROW_F = 80
ROWS_ALL = 112

REACH = 4
OFFSETS = tuple(sign * k for k in range(1, REACH + 1) for sign in (1, -1))
BLK_STEPS = (1, -1, 2, -2)

G0, G1, G2, H1, G3, G4, H2 = range(7)
GROUPS_NEAR = {1: G1, 2: G2, 3: G3, 4: G4}
GROUPS_OUTER = {1: H1, 2: H2}
STAGE_GROUPS = (5, 3, 2, 1)
STAGE_DOMAINS = (7, 5, 3, 1)
DOMAINS = (0, 1, -1, 2, -2, 3, -3)


def slot_of(offset):
    return 2 * (abs(offset) - 1) + (offset < 0)


def upper_half(domain):
    if domain == 0:
        return G0
    return GROUPS_OUTER[domain] if domain > 0 else GROUPS_NEAR[-domain]


def lower_half(domain):
    if domain == 0:
        return G0
    return GROUPS_NEAR[domain] if domain > 0 else GROUPS_OUTER[-domain]


def windows_of(domain):
    result = []
    for w in range(4):
        near = domain - 1 if w < 2 else domain + 1
        group = upper_half(near) if w < 2 else lower_half(near)
        first = 4 if w < 2 else 0
        slot = 0 if near == 0 else 1 + slot_of(near)
        tile = 2 + w if w < 2 else w - 2
        served = []
        for half, cell in ((lower_half, w), (upper_half, 4 + w)):
            if abs(domain) in (0, 1) or half is (lower_half if domain > 0 else upper_half):
                served.append((half(domain), cell))
        result.append((group, first, slot, tile, served))
    return result


GATHER = lax.GatherDimensionNumbers(
    offset_dims=(),
    collapsed_slice_dims=(1,),
    start_index_map=(1,),
    operand_batching_dims=(0,),
    start_indices_batching_dims=(0,),
)


def take_lanes(rows, lane):
    return lax.gather(
        rows,
        lane[..., None],
        GATHER,
        slice_sizes=(1, 1),
        mode=lax.GatherScatterMode.PROMISE_IN_BOUNDS,
    )


def split3(value):
    high = value.astype(BF16)
    rest = value - high.astype(F32)
    mid = rest.astype(BF16)
    low = (rest - mid.astype(F32)).astype(BF16)
    return high.astype(F32), mid.astype(F32), low.astype(F32)


def fold_cells(parts, row):
    def join(a, b, mask, turn):
        return jnp.where(mask, a, b) + pltpu.roll(jnp.where(mask, b, a), turn, 0)

    def turned(start):
        return jnp.bitwise_and(row - start, 7)

    pairs = [join(parts[s], parts[s + 4], turned(s) < 4, 4) for s in range(4)]
    quads = [
        join(pairs[s], pairs[s + 2], jnp.bitwise_and(turned(s), 2) == 0, 6) for s in range(2)
    ]
    return join(quads[0], quads[1], jnp.bitwise_and(row, 1) == 0, 7)


def kernel(
    n_blk,
    n_dom,
    pos_hbm,
    lin_hbm,
    bur_hbm,
    mob_hbm,
    clo_hbm,
    map_hbm,
    new_ref,
    vel_ref,
    pos_v,
    lin_v,
    bur_v,
    mob_v,
    far_blk,
    dom_in,
    force_in,
    group,
    close,
    maps,
    map_all,
    feat,
    lhs,
    acc,
    statics_gh,
    weight_own,
    weight,
    ghost,
    frow,
    vfirst,
    xnow,
    xguess,
    xsend,
    xrecv,
    local_sem,
    send_sem,
    recv_sem,
):
    me_b = lax.axis_index("blk")
    me_d = lax.axis_index("dom")

    def peer(db, dd):
        return {
            "blk": lax.rem(me_b + db + n_blk, n_blk),
            "dom": lax.rem(me_d + dd + n_dom, n_dom),
        }

    local = []
    for i, (src, dst) in enumerate(
        (
            (pos_hbm, pos_v),
            (lin_hbm, lin_v),
            (bur_hbm, bur_v),
            (mob_hbm, mob_v),
            (clo_hbm, close.at[G0]),
            (map_hbm, maps.at[0]),
        )
    ):
        copy = pltpu.make_async_copy(src, dst, local_sem.at[i])
        copy.start()
        local.append(copy)

    barrier = pltpu.get_barrier_semaphore()
    for step in BLK_STEPS:
        pl.semaphore_signal(barrier, inc=1, device_id=peer(step, 0), device_id_type=MESH)
    for step in OFFSETS:
        pl.semaphore_signal(barrier, inc=1, device_id=peer(0, step), device_id_type=MESH)

    for copy in local[:4]:
        copy.wait()
    state = group.at[G0]
    for first, ref in ((0, pos_v), (24, lin_v), (48, bur_v), (72, mob_v)):
        for k in range(ref.shape[0]):
            for q in range(CELLS):
                state[pl.ds(first + k * 8 + q, 1), :] = ref[pl.ds(k, 1), pl.ds(q * LANES, LANES)]

    pl.semaphore_wait(barrier, len(BLK_STEPS) + len(OFFSETS))

    sends = []

    def send(src, dst, device):
        i = len(sends)
        copy = pltpu.make_async_remote_copy(
            src_ref=src,
            dst_ref=dst,
            send_sem=send_sem.at[i],
            recv_sem=recv_sem.at[i],
            device_id=device,
            device_id_type=MESH,
        )
        copy.start()
        sends.append(copy)
        return copy

    blk_copies = [
        send(state.at[pl.ds(0, 72)], far_blk.at[i], peer(step, 0))
        for i, step in enumerate(BLK_STEPS)
    ]
    dom_copies = []
    for offset in OFFSETS:
        dom_copies.append(
            send(
                state.at[pl.ds(0, ROWS_SETUP)],
                dom_in.at[slot_of(offset)],
                peer(0, -offset),
            )
        )
    for offset in OFFSETS:
        dom_copies.append(send(map_hbm, maps.at[1 + slot_of(offset)], peer(0, -offset)))
    for offset in OFFSETS[:6]:
        halves = (0, 1) if abs(offset) == 1 else ((0,) if offset > 0 else (1,))
        for half in halves:
            target = (lower_half, upper_half)[half](offset)
            cols = pl.ds(half * 512, 512)
            dom_copies.append(
                send(clo_hbm.at[:, cols], close.at[target, :, cols], peer(0, -offset))
            )

    own_pos = [state[pl.ds(8 * k, 8), :] for k in range(3)]
    centres = [jnp.mean(rows, axis=1, keepdims=True) for rows in own_pos]
    one = jnp.ones((8, LANES), F32)
    zero = jnp.zeros((8, LANES), F32)

    def put_features(rows_of, target):
        pos = [rows_of(k) - centres[k] for k in range(3)]
        line = [rows_of(3 + k) for k in range(3)]
        burg = [rows_of(6 + k) for k in range(3)]
        square = pos[0] * pos[0] + pos[1] * pos[1] + pos[2] * pos[2]
        products = [b * l for b in burg for l in line]
        if target:
            rest = [-2.0 * p for p in pos] + [square, one, zero, zero]
        else:
            rest = pos + [one, square + LONG_CORE * LONG_CORE, zero, zero]
            for k in range(3):
                feat[1, pl.ds(8 * k, 8), :] = pos[k]
        for f, value in enumerate(products + rest):
            for piece, part in enumerate(split3(value)):
                feat[0, pl.ds((piece * 16 + f) * 8, 8), :] = part

    put_features(lambda k: state[pl.ds(8 * k, 8), :], True)
    numerator_row = lax.broadcasted_iota(jnp.int32, (16, LANES), 0) < 9

    def build(q, carry):
        part = [feat[0, pl.ds(piece * 128 + q, 16, stride=8), :] for piece in range(3)]
        for half in range(2):
            keep = numerator_row if half == 0 else jnp.logical_not(numerator_row)
            rows = jnp.concatenate(
                [jnp.where(keep, part[i], 0.0) for i in (0, 0, 1, 0, 1, 2)]
                + [jnp.zeros((32, LANES), F32)],
                axis=0,
            )
            lhs[q, pl.ds(half * LANES, LANES), :] = rows.T.astype(BF16)
        return carry

    lax.fori_loop(0, CELLS, build, 0)

    def long_block(source_rows, s):
        put_features(source_rows, False)

        def cell(q, carry):
            part = [feat[0, pl.ds(piece * 128 + q, 16, stride=8), :] for piece in range(3)]
            rhs = jnp.concatenate(
                [part[i] for i in (0, 1, 0, 2, 1, 0)] + [jnp.zeros((32, LANES), F32)], axis=0
            ).astype(BF16)
            both = jnp.dot(lhs[q], rhs, preferred_element_type=F32)
            inverse = lax.rsqrt(both[LANES:])
            w = both[:LANES] * inverse * (inverse * inverse)
            for k in range(4):
                term = w if k == 3 else w * feat[1, pl.ds(8 * k + q, 1), :]
                if s == 0:
                    acc[q, k] = term
                else:
                    acc[q, k] += term
            return carry

        lax.fori_loop(0, CELLS, cell, 0, unroll=2)

    long_block(lambda k: state[pl.ds(8 * k, 8), :], 0)
    for i in range(4):
        blk_copies[i].wait_recv()
        long_block(lambda k: far_blk[i, pl.ds(8 * k, 8), :], i + 1)

    lane_id = lax.broadcasted_iota(jnp.int32, (LANES, LANES), 1)

    def reduce_cell(q, columns):
        for k in range(4):
            total = jnp.sum(acc[q, k], axis=1, keepdims=True)
            columns = jnp.where(lane_id == k * 8 + q, total, columns)
        return columns

    columns = lax.fori_loop(
        0, CELLS, reduce_cell, jnp.zeros((LANES, LANES), F32), unroll=2
    )
    sums = columns.T
    scale = 1.0 / math.sqrt(5 * LANES)
    for k in range(3):
        force = ((own_pos[k] - centres[k]) * sums[24:32] - sums[8 * k : 8 * k + 8]) * scale
        state[pl.ds(ROW_F + 8 * k, 8), :] = force
    force_copies = [
        send(state.at[pl.ds(ROW_F, 24)], force_in.at[slot_of(offset)], peer(0, -offset))
        for offset in OFFSETS[:6]
    ]

    row = lax.broadcasted_iota(jnp.int32, (8, LANES), 0)
    low_half = row < 4
    for copy in local[4:]:
        copy.wait()
    for copy in dom_copies:
        copy.wait_recv()

    def merge(source, rows, k, outer):
        above, below = source[slot_of(k), rows, :], source[slot_of(-k), rows, :]
        if outer:
            return jnp.where(low_half, below, above)
        return jnp.where(low_half, above, below)

    merged_groups = [(g, k, False) for k, g in GROUPS_NEAR.items()] + [
        (g, k, True) for k, g in GROUPS_OUTER.items()
    ]
    for g, k, outer in merged_groups:
        for c in range(10):
            rows = pl.ds(8 * c, 8)
            group[g, rows, :] = merge(dom_in, rows, k, outer)
    for slot in range(9):
        for j in range(4):
            map_all[pl.ds((slot * 4 + j) * SUBS, SUBS), :] = maps[slot, :, pl.ds(j * LANES, LANES)]
    for g in range(7):
        xnow[g, pl.ds(0, 24), :] = group[g, pl.ds(0, 24), :]

    def pick_windows(t, n_domains, n_groups, tile_of, target):
        for domain in DOMAINS[:n_domains]:
            for g, first, slot, tile, served in windows_of(domain):
                place = map_all[pl.ds((slot * 4 + tile) * SUBS + t, 1), :]
                place = jnp.broadcast_to(place, (8, LANES))
                lane = place & 127
                at = (place >> 7) & 3
                picked = [take_lanes(tile_of(g, first + i), lane) for i in range(4)]
                odd = (at & 1) != 0
                result = jnp.where(
                    at >= 2,
                    jnp.where(odd, picked[3], picked[2]),
                    jnp.where(odd, picked[1], picked[0]),
                )
                for g_to, cell in served:
                    if g_to < n_groups:
                        target[pl.ds((g_to * 8 + cell) * 8, 8), :] = result

    def spread(value):
        return jnp.broadcast_to(value, (8, LANES))

    def close_of(g, s, r):
        return close[g, pl.ds(8 * r, 8), pl.ds(s * LANES, LANES)]

    def dots(mine, other):
        line = mine[0] * other[0] + mine[1] * other[1] + mine[2] * other[2]
        burg = mine[3] * other[3] + mine[4] * other[4] + mine[5] * other[5]
        return line * burg

    def static_rows(g, s):
        return [spread(group[g, pl.ds(24 + 8 * k + s, 1), :]) for k in range(6)]

    def weights_own(g, carry):
        for s in range(CELLS):
            mine = static_rows(g, s)
            for r in range(4):
                index = close_of(g, s, r)
                lane = index & 127
                other = [take_lanes(m, lane) for m in mine]
                weight_own[g, s, pl.ds(8 * r, 8), :] = jnp.where(
                    index < LANES, dots(mine, other), 0.0
                )
        return carry

    lax.fori_loop(0, 5, weights_own, 0)

    def static_tile(g, s):
        return group[g, pl.ds(24 + s, 8, stride=8), :]

    def weights_ghost(t, n_domains, n_groups):
        pick_windows(t, n_domains, n_groups, static_tile, statics_gh)

        def one(g, carry):
            for s in range(CELLS):
                mine = static_rows(g, s)
                base = (g * 8 + s) * 8
                theirs = [spread(statics_gh[pl.ds(base + k, 1), :]) for k in range(6)]
                for r in range(4):
                    index = close_of(g, s, r)
                    lane = index & 127
                    other = [take_lanes(m, lane) for m in theirs]
                    value = jnp.where(index < 2 * LANES, dots(mine, other), 0.0)
                    rows = pl.ds(8 * r, 8)
                    weight[t, g, s, rows, :] = jnp.where(
                        index < LANES, weight_own[g, s, rows, :], value
                    )
            return carry

        lax.fori_loop(0, n_groups, one, 0)

    short_scale = 1.0 / math.sqrt(SLOTS)

    def tiles_in(positions):
        return lambda g, s: positions[g, pl.ds(s, 8, stride=8), :]

    def evaluate(t, stage, positions):
        n_groups = STAGE_GROUPS[stage]
        pick_windows(t, STAGE_DOMAINS[stage], n_groups, tiles_in(positions), ghost)

        def one(g, carry):
            sums = [[], [], []]
            for s in range(CELLS):
                mine = [spread(positions[g, pl.ds(8 * k + s, 1), :]) for k in range(3)]
                base = (g * 8 + s) * 8
                theirs = [spread(ghost[pl.ds(base + k, 1), :]) for k in range(3)]
                total = None
                for r in range(4):
                    index = close_of(g, s, r)
                    lane = index & 127
                    is_ghost = index >= LANES
                    inner = [take_lanes(m, lane) for m in mine]
                    outer = [take_lanes(m, lane) for m in theirs]
                    delta = [
                        m - jnp.where(is_ghost, o, i) for m, o, i in zip(mine, outer, inner)
                    ]
                    radius = (
                        delta[0] * delta[0]
                        + delta[1] * delta[1]
                        + delta[2] * delta[2]
                        + SHORT_CORE * SHORT_CORE
                    )
                    inverse = lax.rsqrt(radius)
                    w = weight[t, g, s, pl.ds(8 * r, 8), :] * inverse * (inverse * inverse)
                    terms = [w * d for d in delta]
                    total = terms if total is None else [a + b for a, b in zip(total, terms)]
                for k in range(3):
                    sums[k].append(total[k])
            for k in range(3):
                frow[g, pl.ds(8 * k, 8), :] = fold_cells(sums[k], row)
            return carry

        lax.fori_loop(0, n_groups, one, 0)

    def drift(g, k):
        rows = pl.ds(8 * k, 8)
        force = group[g, pl.ds(ROW_F + 8 * k, 8), :] + frow[g, rows, :] * short_scale
        return group[g, pl.ds(ROW_MOB, 8), :] * force

    def make_guess(n_groups):
        for g in range(n_groups):
            for k in range(3):
                rows = pl.ds(8 * k, 8)
                first = drift(g, k)
                vfirst[g, rows, :] = first
                xguess[g, rows, :] = xnow[g, rows, :] + STEP * first

    def advance(n_groups, last):
        for g in range(n_groups):
            for k in range(3):
                rows = pl.ds(8 * k, 8)
                velocity = 0.5 * (vfirst[g, rows, :] + drift(g, k))
                position = xnow[g, rows, :] + STEP * velocity
                if last:
                    for q in range(CELLS):
                        cols = pl.ds(q * LANES, LANES)
                        new_ref[pl.ds(k, 1), cols] = position[q : q + 1, :]
                        vel_ref[pl.ds(k, 1), cols] = velocity[q : q + 1, :]
                else:
                    xnow[g, rows, :] = position

    def finish_block(t, last):
        evaluate(t, 1, xguess)
        advance(3, False)
        evaluate(t + 1, 2, xnow)
        make_guess(2)
        evaluate(t + 1, 3, xguess)
        advance(1, last)

    weights_ghost(0, 7, 5)
    evaluate(0, 0, xnow)
    weights_ghost(1, 3, 2)
    for copy in force_copies:
        copy.wait_recv()
    for g, k, outer in ((G1, 1, False), (H1, 1, True), (G2, 2, False), (G3, 3, False)):
        for c in range(3):
            group[g, pl.ds(ROW_F + 8 * c, 8), :] = merge(force_in, pl.ds(8 * c, 8), k, outer)
    make_guess(5)
    finish_block(0, False)

    xsend[...] = xnow[G0, pl.ds(0, 24), :]
    x_copies = [
        send(xsend, xrecv.at[slot_of(offset)], peer(0, -offset)) for offset in OFFSETS
    ]
    weights_ghost(2, 7, 5)
    weights_ghost(3, 3, 2)
    for copy in x_copies:
        copy.wait_recv()
    for g, k, outer in merged_groups:
        for c in range(3):
            rows = pl.ds(8 * c, 8)
            xnow[g, rows, :] = merge(xrecv, rows, k, outer)
    evaluate(2, 0, xnow)
    make_guess(5)
    finish_block(2, True)

    for copy in sends:
        copy.wait_send()


def solution(mesh):
    n_blk, n_dom = mesh.shape["blk"], mesh.shape["dom"]

    def step(positions, line_vectors, burgers, mobility, close_list, ghost_map):
        count = positions.shape[1]
        anywhere = pl.BlockSpec(memory_space=pl.ANY)
        vmem = pl.BlockSpec(memory_space=pltpu.VMEM)
        shape = jax.ShapeDtypeStruct((3, count), F32)
        n_sends = 4 + 8 + 8 + 8 + 6 + 8
        return pl.pallas_call(
            functools.partial(kernel, n_blk, n_dom),
            out_shape=(shape, shape),
            in_specs=[anywhere] * 6,
            out_specs=(vmem, vmem),
            scratch_shapes=[
                pltpu.VMEM((3, count), F32),
                pltpu.VMEM((3, count), F32),
                pltpu.VMEM((3, count), F32),
                pltpu.VMEM((1, count), F32),
                pltpu.VMEM((4, 72, LANES), F32),
                pltpu.VMEM((8, ROWS_SETUP, LANES), F32),
                pltpu.VMEM((6, 24, LANES), F32),
                pltpu.VMEM((7, ROWS_ALL, LANES), F32),
                pltpu.VMEM((5, SLOTS, count), jnp.int32),
                pltpu.VMEM((9, SUBS, 512), jnp.int32),
                pltpu.VMEM((144, LANES), jnp.int32),
                pltpu.VMEM((2, 384, LANES), F32),
                pltpu.VMEM((CELLS, 256, LANES), BF16),
                pltpu.VMEM((CELLS, 4, LANES, LANES), F32),
                pltpu.VMEM((320, LANES), F32),
                pltpu.VMEM((5, CELLS, SLOTS, LANES), F32),
                pltpu.VMEM((SUBS, 5, CELLS, SLOTS, LANES), F32),
                pltpu.VMEM((320, LANES), F32),
                pltpu.VMEM((5, 24, LANES), F32),
                pltpu.VMEM((5, 24, LANES), F32),
                pltpu.VMEM((7, 64, LANES), F32),
                pltpu.VMEM((5, 64, LANES), F32),
                pltpu.VMEM((24, LANES), F32),
                pltpu.VMEM((8, 24, LANES), F32),
                pltpu.SemaphoreType.DMA((6,)),
                pltpu.SemaphoreType.DMA((n_sends,)),
                pltpu.SemaphoreType.DMA((n_sends,)),
            ],
            compiler_params=pltpu.CompilerParams(collective_id=0, has_side_effects=True),
        )(positions, line_vectors, burgers, mobility.reshape(1, count), close_list, ghost_map)

    both = ("blk", "dom")
    return jax.shard_map(
        step,
        mesh=mesh,
        in_specs=(
            P(None, both),
            P(None, both),
            P(None, both),
            P(both),
            P(None, both),
            P(None, both),
        ),
        out_specs=(P(None, both), P(None, both)),
        check_vma=False,
    )
```

```python
import functools
import math

import jax
import jax.numpy as jnp
from jax import lax
from jax.experimental import pallas as pl
from jax.experimental.pallas import tpu as pltpu
from jax.sharding import PartitionSpec as P

MESH = pl.DeviceIdType.MESH
F32 = jnp.float32
BF16 = jnp.bfloat16

LANES = 128
CELLS = 8
SLOTS = 32
SUBS = 4
LONG_CORE = 1.0
SHORT_CORE = 0.25
STEP = 0.05

ROWS_SETUP = 80
ROW_MOB = 72
ROW_F = 80
ROWS_ALL = 112

REACH = 4
OFFSETS = tuple(sign * k for k in range(1, REACH + 1) for sign in (1, -1))
BLK_STEPS = (1, -1, 2, -2)

G0, G1, G2, H1, G3, G4, H2 = range(7)
GROUPS_NEAR = {1: G1, 2: G2, 3: G3, 4: G4}
GROUPS_OUTER = {1: H1, 2: H2}
DOMAINS_FOR = {1: 1, 2: 3, 3: 5, 5: 7}
DOMAINS = (0, 1, -1, 2, -2, 3, -3)


def slot_of(offset):
    return 2 * (abs(offset) - 1) + (offset < 0)


def upper_half(domain):
    if domain == 0:
        return G0
    return GROUPS_OUTER[domain] if domain > 0 else GROUPS_NEAR[-domain]


def lower_half(domain):
    if domain == 0:
        return G0
    return GROUPS_NEAR[domain] if domain > 0 else GROUPS_OUTER[-domain]


def windows_of(domain):
    result = []
    for w in range(4):
        near = domain - 1 if w < 2 else domain + 1
        group = upper_half(near) if w < 2 else lower_half(near)
        first = 4 if w < 2 else 0
        slot = 0 if near == 0 else 1 + slot_of(near)
        tile = 2 + w if w < 2 else w - 2
        served = []
        for half, cell in ((lower_half, w), (upper_half, 4 + w)):
            if abs(domain) in (0, 1) or half is (lower_half if domain > 0 else upper_half):
                served.append((half(domain), cell))
        result.append((group, first, slot, tile, served))
    return result


GATHER = lax.GatherDimensionNumbers(
    offset_dims=(),
    collapsed_slice_dims=(1,),
    start_index_map=(1,),
    operand_batching_dims=(0,),
    start_indices_batching_dims=(0,),
)


def take_lanes(rows, lane):
    return lax.gather(
        rows,
        lane[..., None],
        GATHER,
        slice_sizes=(1, 1),
        mode=lax.GatherScatterMode.PROMISE_IN_BOUNDS,
    )


def split3(value):
    high = value.astype(BF16)
    rest = value - high.astype(F32)
    mid = rest.astype(BF16)
    low = (rest - mid.astype(F32)).astype(BF16)
    return high.astype(F32), mid.astype(F32), low.astype(F32)


def fold_cells(parts, row):
    def join(a, b, mask, turn):
        return jnp.where(mask, a, b) + pltpu.roll(jnp.where(mask, b, a), turn, 0)

    def turned(start):
        return jnp.bitwise_and(row - start, 7)

    pairs = [join(parts[s], parts[s + 4], turned(s) < 4, 4) for s in range(4)]
    quads = [
        join(pairs[s], pairs[s + 2], jnp.bitwise_and(turned(s), 2) == 0, 6) for s in range(2)
    ]
    return join(quads[0], quads[1], jnp.bitwise_and(row, 1) == 0, 7)


def kernel(
    n_blk,
    n_dom,
    pos_hbm,
    lin_hbm,
    bur_hbm,
    mob_hbm,
    clo_hbm,
    map_hbm,
    pos_out,
    vel_out,
    pos_v,
    lin_v,
    bur_v,
    mob_v,
    far_blk,
    dom_in,
    group,
    close,
    maps,
    map_all,
    feat,
    lhs,
    acc,
    statics_gh,
    weight_own,
    weight,
    ghost,
    frow,
    vfirst,
    xnow,
    xguess,
    xhalf,
    msend,
    mrecv,
    xsend,
    xrecv,
    local_sem,
    send_sem,
    recv_sem,
):
    me_b = lax.axis_index("blk")
    me_d = lax.axis_index("dom")

    def peer(db, dd):
        return {
            "blk": lax.rem(me_b + db + n_blk, n_blk),
            "dom": lax.rem(me_d + dd + n_dom, n_dom),
        }

    local = []
    for i, (src, dst) in enumerate(
        (
            (pos_hbm, pos_v),
            (lin_hbm, lin_v),
            (bur_hbm, bur_v),
            (mob_hbm, mob_v),
            (clo_hbm, close.at[G0]),
            (map_hbm, maps.at[0]),
        )
    ):
        copy = pltpu.make_async_copy(src, dst, local_sem.at[i])
        copy.start()
        local.append(copy)

    barrier = pltpu.get_barrier_semaphore()
    for step in BLK_STEPS:
        pl.semaphore_signal(barrier, inc=1, device_id=peer(step, 0), device_id_type=MESH)
    for step in OFFSETS:
        pl.semaphore_signal(barrier, inc=1, device_id=peer(0, step), device_id_type=MESH)

    for copy in local[:4]:
        copy.wait()
    state = group.at[G0]
    for first, ref in ((0, pos_v), (24, lin_v), (48, bur_v), (72, mob_v)):
        for k in range(ref.shape[0]):
            for q in range(CELLS):
                state[pl.ds(first + k * 8 + q, 1), :] = ref[pl.ds(k, 1), pl.ds(q * LANES, LANES)]

    pl.semaphore_wait(barrier, len(BLK_STEPS) + len(OFFSETS))

    sends = []

    def send(src, dst, device):
        i = len(sends)
        copy = pltpu.make_async_remote_copy(
            src_ref=src,
            dst_ref=dst,
            send_sem=send_sem.at[i],
            recv_sem=recv_sem.at[i],
            device_id=device,
            device_id_type=MESH,
        )
        copy.start()
        sends.append(copy)
        return copy

    blk_copies = [
        send(state.at[pl.ds(0, 72)], far_blk.at[i], peer(step, 0))
        for i, step in enumerate(BLK_STEPS)
    ]

    def send_state(k):
        pairs = (k, -k)
        return [
            send(state.at[pl.ds(0, ROWS_SETUP)], dom_in.at[slot_of(o)], peer(0, -o)) for o in pairs
        ] + [send(map_hbm, maps.at[1 + slot_of(o)], peer(0, -o)) for o in pairs]

    def send_close(target, k, outer):
        result = []
        for o in (k, -k):
            cols = pl.ds(512 * ((o > 0) == outer), 512)
            result.append(send(clo_hbm.at[:, cols], close.at[target, :, cols], peer(0, -o)))
        return result

    copies_first = send_state(1)
    copies_second = (
        send_state(2) + send_close(G1, 1, False) + send_state(3) + send_close(G2, 2, False)
    )
    copies_third = send_close(H1, 1, True) + send_close(G3, 3, False) + send_state(4)

    own_pos = [state[pl.ds(8 * k, 8), :] for k in range(3)]
    centres = [jnp.mean(rows, axis=1, keepdims=True) for rows in own_pos]
    one = jnp.ones((8, LANES), F32)
    zero = jnp.zeros((8, LANES), F32)

    def put_features(rows_of, target):
        pos = [rows_of(k) - centres[k] for k in range(3)]
        line = [rows_of(3 + k) for k in range(3)]
        burg = [rows_of(6 + k) for k in range(3)]
        square = pos[0] * pos[0] + pos[1] * pos[1] + pos[2] * pos[2]
        products = [b * l for b in burg for l in line]
        if target:
            rest = [-2.0 * p for p in pos] + [square, one, zero, zero]
        else:
            rest = pos + [one, square + LONG_CORE * LONG_CORE, zero, zero]
            for k in range(3):
                feat[1, pl.ds(8 * k, 8), :] = pos[k]
        for f, value in enumerate(products + rest):
            for piece, part in enumerate(split3(value)):
                feat[0, pl.ds((piece * 16 + f) * 8, 8), :] = part

    put_features(lambda k: state[pl.ds(8 * k, 8), :], True)
    numerator_row = lax.broadcasted_iota(jnp.int32, (16, LANES), 0) < 9

    def build(q, carry):
        part = [feat[0, pl.ds(piece * 128 + q, 16, stride=8), :] for piece in range(3)]
        for half in range(2):
            keep = numerator_row if half == 0 else jnp.logical_not(numerator_row)
            rows = jnp.concatenate(
                [jnp.where(keep, part[i], 0.0) for i in (0, 0, 1, 0, 1, 2)]
                + [jnp.zeros((32, LANES), F32)],
                axis=0,
            )
            lhs[q, pl.ds(half * LANES, LANES), :] = rows.T.astype(BF16)
        return carry

    lax.fori_loop(0, CELLS, build, 0)

    def long_block(source_rows, s):
        put_features(source_rows, False)

        def cell(q, carry):
            part = [feat[0, pl.ds(piece * 128 + q, 16, stride=8), :] for piece in range(3)]
            rhs = jnp.concatenate(
                [part[i] for i in (0, 1, 0, 2, 1, 0)] + [jnp.zeros((32, LANES), F32)], axis=0
            ).astype(BF16)
            both = jnp.dot(lhs[q], rhs, preferred_element_type=F32)
            inverse = lax.rsqrt(both[LANES:])
            w = both[:LANES] * inverse * (inverse * inverse)
            for k in range(4):
                term = w if k == 3 else w * feat[1, pl.ds(8 * k + q, 1), :]
                if s == 0:
                    acc[q, k] = term
                else:
                    acc[q, k] += term
            return carry

        lax.fori_loop(0, CELLS, cell, 0, unroll=2)

    long_block(lambda k: state[pl.ds(8 * k, 8), :], 0)
    row = lax.broadcasted_iota(jnp.int32, (8, LANES), 0)
    low_half = row < 4

    def merge(source, rows, k, outer):
        above, below = source[slot_of(k), rows, :], source[slot_of(-k), rows, :]
        if outer:
            return jnp.where(low_half, below, above)
        return jnp.where(low_half, above, below)

    near = {G1: (1, False), G2: (2, False), H1: (1, True), G3: (3, False), G4: (4, False), H2: (2, True)}

    def merge_into(target, first, source, source_first, components, groups):
        for g in groups:
            k, outer = near[g]
            for c in range(components):
                target[g, pl.ds(first + 8 * c, 8), :] = merge(
                    source, pl.ds(source_first + 8 * c, 8), k, outer
                )

    def put_maps(slots):
        for slot in slots:
            for j in range(4):
                map_all[pl.ds((slot * 4 + j) * SUBS, SUBS), :] = maps[
                    slot, :, pl.ds(j * LANES, LANES)
                ]

    def pick_windows(t, n_domains, n_groups, tile_of, target, start=0):
        for domain in DOMAINS[start:n_domains]:
            for g, first, slot, tile, served in windows_of(domain):
                place = map_all[pl.ds((slot * 4 + tile) * SUBS + t, 1), :]
                place = jnp.broadcast_to(place, (8, LANES))
                lane = place & 127
                at = (place >> 7) & 3
                picked = [take_lanes(tile_of(g, first + i), lane) for i in range(4)]
                odd = (at & 1) != 0
                result = jnp.where(
                    at >= 2,
                    jnp.where(odd, picked[3], picked[2]),
                    jnp.where(odd, picked[1], picked[0]),
                )
                for g_to, cell in served:
                    if g_to < n_groups:
                        target[pl.ds((g_to * 8 + cell) * 8, 8), :] = result

    def spread(value):
        return jnp.broadcast_to(value, (8, LANES))

    def close_of(g, s, r):
        return close[g, pl.ds(8 * r, 8), pl.ds(s * LANES, LANES)]

    def dots(mine, other):
        line = mine[0] * other[0] + mine[1] * other[1] + mine[2] * other[2]
        burg = mine[3] * other[3] + mine[4] * other[4] + mine[5] * other[5]
        return line * burg

    def static_rows(g, s):
        return [spread(group[g, pl.ds(24 + 8 * k + s, 1), :]) for k in range(6)]

    def weights_own(g, carry):
        for s in range(CELLS):
            mine = static_rows(g, s)
            for r in range(4):
                index = close_of(g, s, r)
                lane = index & 127
                other = [take_lanes(m, lane) for m in mine]
                weight_own[g, s, pl.ds(8 * r, 8), :] = jnp.where(
                    index < LANES, dots(mine, other), 0.0
                )
        return carry

    def static_tile(g, s):
        return group[g, pl.ds(24 + s, 8, stride=8), :]

    def weights_ghost(t, n_groups, start=0):
        pick_windows(t, DOMAINS_FOR[n_groups], n_groups, static_tile, statics_gh, start)

        def one(g, carry):
            for s in range(CELLS):
                mine = static_rows(g, s)
                base = (g * 8 + s) * 8
                theirs = [spread(statics_gh[pl.ds(base + k, 1), :]) for k in range(6)]
                for r in range(4):
                    index = close_of(g, s, r)
                    lane = index & 127
                    other = [take_lanes(m, lane) for m in theirs]
                    value = jnp.where(index < 2 * LANES, dots(mine, other), 0.0)
                    rows = pl.ds(8 * r, 8)
                    weight[t, g, s, rows, :] = jnp.where(
                        index < LANES, weight_own[g, s, rows, :], value
                    )
            return carry

        lax.fori_loop(start, n_groups, one, 0)

    short_scale = 1.0 / math.sqrt(SLOTS)

    def tiles_in(positions):
        return lambda g, s: positions[g, pl.ds(s, 8, stride=8), :]

    def evaluate(t, n_groups, positions):
        pick_windows(t, DOMAINS_FOR[n_groups], n_groups, tiles_in(positions), ghost)

        def one(g, carry):
            sums = [[], [], []]
            for s in range(CELLS):
                mine = [spread(positions[g, pl.ds(8 * k + s, 1), :]) for k in range(3)]
                base = (g * 8 + s) * 8
                theirs = [spread(ghost[pl.ds(base + k, 1), :]) for k in range(3)]
                total = None
                for r in range(4):
                    index = close_of(g, s, r)
                    lane = index & 127
                    is_ghost = index >= LANES
                    inner = [take_lanes(m, lane) for m in mine]
                    outer = [take_lanes(m, lane) for m in theirs]
                    delta = [
                        m - jnp.where(is_ghost, o, i) for m, o, i in zip(mine, outer, inner)
                    ]
                    radius = (
                        delta[0] * delta[0]
                        + delta[1] * delta[1]
                        + delta[2] * delta[2]
                        + SHORT_CORE * SHORT_CORE
                    )
                    inverse = lax.rsqrt(radius)
                    w = weight[t, g, s, pl.ds(8 * r, 8), :] * inverse * (inverse * inverse)
                    terms = [w * d for d in delta]
                    total = terms if total is None else [a + b for a, b in zip(total, terms)]
                for k in range(3):
                    sums[k].append(total[k])
            for k in range(3):
                frow[g, pl.ds(8 * k, 8), :] = fold_cells(sums[k], row)
            return carry

        lax.fori_loop(0, n_groups, one, 0)

    def drift(g, k):
        rows = pl.ds(8 * k, 8)
        force = group[g, pl.ds(ROW_F + 8 * k, 8), :] + frow[g, rows, :] * short_scale
        return group[g, pl.ds(ROW_MOB, 8), :] * force

    def make_guess(n_groups):
        for g in range(n_groups):
            for k in range(3):
                rows = pl.ds(8 * k, 8)
                first = drift(g, k)
                position = xnow[g, rows, :]
                vfirst[g, rows, :] = first
                xguess[g, rows, :] = position + STEP * first
                xhalf[g, rows, :] = position + (0.5 * STEP) * first

    def advance(n_groups):
        for g in range(n_groups):
            for k in range(3):
                rows = pl.ds(8 * k, 8)
                xnow[g, rows, :] = xhalf[g, rows, :] + (0.5 * STEP) * drift(g, k)

    for copy in local[4:]:
        copy.wait()
    lax.fori_loop(0, 1, weights_own, 0)
    put_maps((0,))
    for i in range(4):
        blk_copies[i].wait_recv()
        long_block(lambda k: far_blk[i, pl.ds(8 * k, 8), :], i + 1)

    lane_id = lax.broadcasted_iota(jnp.int32, (LANES, LANES), 1)

    def reduce_cell(q, columns):
        for k in range(4):
            total = jnp.sum(acc[q, k], axis=1, keepdims=True)
            columns = jnp.where(lane_id == k * 8 + q, total, columns)
        return columns

    columns = lax.fori_loop(
        0, CELLS, reduce_cell, jnp.zeros((LANES, LANES), F32), unroll=2
    )
    sums = columns.T
    scale = 1.0 / math.sqrt(5 * LANES)
    for k in range(3):
        force = ((own_pos[k] - centres[k]) * sums[24:32] - sums[8 * k : 8 * k + 8]) * scale
        state[pl.ds(ROW_F + 8 * k, 8), :] = force


    for copy in copies_first:
        copy.wait_recv()
    merge_into(group, 0, dom_in, 0, 10, (G1, H1))
    put_maps((1, 2))
    xnow[G0, pl.ds(0, 24), :] = state[pl.ds(0, 24), :]
    xnow[G1, pl.ds(0, 24), :] = group[G1, pl.ds(0, 24), :]
    weights_ghost(0, 1)
    evaluate(0, 1, xnow)
    make_guess(1)
    for k in range(3):
        for part, ref in ((0, xguess), (24, xhalf)):
            msend[pl.ds(part + 8 * k, 8), :] = ref[G0, pl.ds(8 * k, 8), :]
        msend[pl.ds(48 + 8 * k, 8), :] = group[G0, pl.ds(ROW_F + 8 * k, 8), :]
    m_copies = [send(msend, mrecv.at[slot_of(o)], peer(0, -o)) for o in OFFSETS[:6]]

    for copy in copies_second:
        copy.wait_recv()
    merge_into(group, 0, dom_in, 0, 10, (G2, G3, H2))
    put_maps((3, 4, 5, 6))
    lax.fori_loop(1, 3, weights_own, 0)
    weights_ghost(0, 3, 1)
    weights_ghost(1, 2)
    for copy in m_copies:
        copy.wait_recv()
    merge_into(xguess, 0, mrecv, 0, 3, (G1, G2, H1, G3))
    merge_into(xhalf, 0, mrecv, 24, 3, (G1, G2))
    merge_into(group, ROW_F, mrecv, 48, 3, (G1, G2, H1, G3))
    evaluate(0, 3, xguess)
    advance(3)
    evaluate(1, 2, xnow)
    make_guess(2)
    evaluate(1, 1, xguess)
    advance(1)
    xsend[...] = xnow[G0, pl.ds(0, 24), :]
    x_copies = [send(xsend, xrecv.at[slot_of(o)], peer(0, -o)) for o in OFFSETS]

    for copy in copies_third:
        copy.wait_recv()
    merge_into(group, 0, dom_in, 0, 10, (G4,))
    put_maps((7, 8))
    lax.fori_loop(3, 5, weights_own, 0)
    weights_ghost(2, 5)
    weights_ghost(3, 2)
    for copy in x_copies:
        copy.wait_recv()
    merge_into(xnow, 0, xrecv, 0, 3, (G1, G2, H1, G3, G4, H2))
    evaluate(2, 5, xnow)
    make_guess(5)
    evaluate(2, 3, xguess)
    advance(3)
    evaluate(3, 2, xnow)
    make_guess(2)
    evaluate(3, 1, xguess)
    for k in range(3):
        twice = vfirst[G0, pl.ds(8 * k, 8), :] + drift(G0, k)
        position = xnow[G0, pl.ds(8 * k, 8), :]
        for q in range(CELLS):
            cols = pl.ds(q * LANES, LANES)
            pos_out[pl.ds(k, 1), cols] = position[q : q + 1, :]
            vel_out[pl.ds(k, 1), cols] = twice[q : q + 1, :]

    for copy in sends:
        copy.wait_send()


def solution(mesh):
    n_blk, n_dom = mesh.shape["blk"], mesh.shape["dom"]

    def step(positions, line_vectors, burgers, mobility, close_list, ghost_map):
        count = positions.shape[1]
        anywhere = pl.BlockSpec(memory_space=pl.ANY)
        vmem = pl.BlockSpec(memory_space=pltpu.VMEM)
        shape = jax.ShapeDtypeStruct((3, count), F32)
        n_sends = 4 + 8 + 8 + 8 + 6 + 8
        base, twice = pl.pallas_call(
            functools.partial(kernel, n_blk, n_dom),
            out_shape=(shape, shape),
            in_specs=[anywhere] * 6,
            out_specs=(vmem, vmem),
            scratch_shapes=[
                pltpu.VMEM((3, count), F32),
                pltpu.VMEM((3, count), F32),
                pltpu.VMEM((3, count), F32),
                pltpu.VMEM((1, count), F32),
                pltpu.VMEM((4, 72, LANES), F32),
                pltpu.VMEM((8, ROWS_SETUP, LANES), F32),
                pltpu.VMEM((7, ROWS_ALL, LANES), F32),
                pltpu.VMEM((5, SLOTS, count), jnp.int32),
                pltpu.VMEM((9, SUBS, 512), jnp.int32),
                pltpu.VMEM((144, LANES), jnp.int32),
                pltpu.VMEM((2, 384, LANES), F32),
                pltpu.VMEM((CELLS, 256, LANES), BF16),
                pltpu.VMEM((CELLS, 4, LANES, LANES), F32),
                pltpu.VMEM((320, LANES), F32),
                pltpu.VMEM((5, CELLS, SLOTS, LANES), F32),
                pltpu.VMEM((SUBS, 5, CELLS, SLOTS, LANES), F32),
                pltpu.VMEM((320, LANES), F32),
                pltpu.VMEM((5, 24, LANES), F32),
                pltpu.VMEM((5, 24, LANES), F32),
                pltpu.VMEM((7, 64, LANES), F32),
                pltpu.VMEM((5, 64, LANES), F32),
                pltpu.VMEM((5, 24, LANES), F32),
                pltpu.VMEM((72, LANES), F32),
                pltpu.VMEM((6, 72, LANES), F32),
                pltpu.VMEM((24, LANES), F32),
                pltpu.VMEM((8, 24, LANES), F32),
                pltpu.SemaphoreType.DMA((6,)),
                pltpu.SemaphoreType.DMA((n_sends,)),
                pltpu.SemaphoreType.DMA((n_sends,)),
            ],
            compiler_params=pltpu.CompilerParams(collective_id=0, has_side_effects=True),
        )(positions, line_vectors, burgers, mobility.reshape(1, count), close_list, ghost_map)
        return base + (0.5 * STEP) * twice, 0.5 * twice

    both = ("blk", "dom")
    return jax.shard_map(
        step,
        mesh=mesh,
        in_specs=(
            P(None, both),
            P(None, both),
            P(None, both),
            P(both),
            P(None, both),
            P(None, both),
        ),
        out_specs=(P(None, both), P(None, both)),
        check_vma=False,
    )
```

```python
import functools
import math

import jax
import jax.numpy as jnp
from jax import lax
from jax.experimental import pallas as pl
from jax.experimental.pallas import tpu as pltpu
from jax.sharding import PartitionSpec as P

MESH = pl.DeviceIdType.MESH
F32 = jnp.float32
BF16 = jnp.bfloat16

LANES = 128
CELLS = 8
PARTS = 4
PART = 32
SLOTS = 32
SUBS = 4
LONG_CORE = 1.0
SHORT_CORE = 0.25
STEP = 0.05

ROWS_SETUP = 80
ROW_MOB = 72
ROW_F = 80
ROWS_ALL = 112

REACH = 4
OFFSETS = tuple(sign * k for k in range(1, REACH + 1) for sign in (1, -1))
BLK_STEPS = (1, -1, 2, -2)

G0, G1, G2, H1, G3, G4, H2 = range(7)
GROUPS_NEAR = {1: G1, 2: G2, 3: G3, 4: G4}
GROUPS_OUTER = {1: H1, 2: H2}
DOMAINS_FOR = {1: 1, 2: 3, 3: 5, 5: 7}
DOMAINS = (0, 1, -1, 2, -2, 3, -3)


def slot_of(offset):
    return 2 * (abs(offset) - 1) + (offset < 0)


def upper_half(domain):
    if domain == 0:
        return G0
    return GROUPS_OUTER[domain] if domain > 0 else GROUPS_NEAR[-domain]


def lower_half(domain):
    if domain == 0:
        return G0
    return GROUPS_NEAR[domain] if domain > 0 else GROUPS_OUTER[-domain]


def windows_of(domain):
    result = []
    for w in range(4):
        near = domain - 1 if w < 2 else domain + 1
        group = upper_half(near) if w < 2 else lower_half(near)
        first = 4 if w < 2 else 0
        slot = 0 if near == 0 else 1 + slot_of(near)
        tile = 2 + w if w < 2 else w - 2
        served = []
        for half, cell in ((lower_half, w), (upper_half, 4 + w)):
            if abs(domain) in (0, 1) or half is (lower_half if domain > 0 else upper_half):
                served.append((half(domain), cell))
        result.append((group, first, slot, tile, served))
    return result


GATHER = lax.GatherDimensionNumbers(
    offset_dims=(),
    collapsed_slice_dims=(1,),
    start_index_map=(1,),
    operand_batching_dims=(0,),
    start_indices_batching_dims=(0,),
)


def take_lanes(rows, lane):
    return lax.gather(
        rows,
        lane[..., None],
        GATHER,
        slice_sizes=(1, 1),
        mode=lax.GatherScatterMode.PROMISE_IN_BOUNDS,
    )


def split3(value):
    high = value.astype(BF16)
    rest = value - high.astype(F32)
    mid = rest.astype(BF16)
    low = (rest - mid.astype(F32)).astype(BF16)
    return high.astype(F32), mid.astype(F32), low.astype(F32)


def fold_cells(parts, row):
    def join(a, b, mask, turn):
        return jnp.where(mask, a, b) + pltpu.roll(jnp.where(mask, b, a), turn, 0)

    def turned(start):
        return jnp.bitwise_and(row - start, 7)

    pairs = [join(parts[s], parts[s + 4], turned(s) < 4, 4) for s in range(4)]
    quads = [
        join(pairs[s], pairs[s + 2], jnp.bitwise_and(turned(s), 2) == 0, 6) for s in range(2)
    ]
    return join(quads[0], quads[1], jnp.bitwise_and(row, 1) == 0, 7)


def kernel(
    n_blk,
    n_dom,
    pos_hbm,
    lin_hbm,
    bur_hbm,
    mob_hbm,
    clo_hbm,
    map_hbm,
    pos_out,
    vel_out,
    pos_v,
    lin_v,
    bur_v,
    mob_v,
    far_blk,
    dom_in,
    group,
    close,
    maps,
    map_all,
    feat,
    feat_pos,
    lhs,
    acc,
    statics_gh,
    weight_own,
    weight,
    ghost,
    frow,
    vfirst,
    xnow,
    xguess,
    xhalf,
    msend,
    mrecv,
    xsend,
    xrecv,
    local_sem,
    send_sem,
    recv_sem,
):
    me_b = lax.axis_index("blk")
    me_d = lax.axis_index("dom")

    def peer(db, dd):
        return {
            "blk": lax.rem(me_b + db + n_blk, n_blk),
            "dom": lax.rem(me_d + dd + n_dom, n_dom),
        }

    local = []
    for i, (src, dst) in enumerate(
        (
            (pos_hbm, pos_v),
            (lin_hbm, lin_v),
            (bur_hbm, bur_v),
            (mob_hbm, mob_v),
            (clo_hbm, close.at[G0]),
            (map_hbm, maps.at[0]),
        )
    ):
        copy = pltpu.make_async_copy(src, dst, local_sem.at[i])
        copy.start()
        local.append(copy)

    barrier = pltpu.get_barrier_semaphore()
    for step in BLK_STEPS:
        pl.semaphore_signal(barrier, inc=1, device_id=peer(step, 0), device_id_type=MESH)
    for step in OFFSETS:
        pl.semaphore_signal(barrier, inc=1, device_id=peer(0, step), device_id_type=MESH)

    for copy in local[:4]:
        copy.wait()
    state = group.at[G0]
    for first, ref in ((0, pos_v), (24, lin_v), (48, bur_v), (72, mob_v)):
        for k in range(ref.shape[0]):
            for q in range(CELLS):
                state[pl.ds(first + k * 8 + q, 1), :] = ref[pl.ds(k, 1), pl.ds(q * LANES, LANES)]

    pl.semaphore_wait(barrier, len(BLK_STEPS) + len(OFFSETS))

    sends = []

    def send(src, dst, device):
        i = len(sends)
        copy = pltpu.make_async_remote_copy(
            src_ref=src,
            dst_ref=dst,
            send_sem=send_sem.at[i],
            recv_sem=recv_sem.at[i],
            device_id=device,
            device_id_type=MESH,
        )
        copy.start()
        sends.append(copy)
        return copy

    blk_copies = [
        send(state.at[pl.ds(0, 72)], far_blk.at[i], peer(step, 0))
        for i, step in enumerate(BLK_STEPS)
    ]

    def send_state(k):
        pairs = (k, -k)
        return [
            send(state.at[pl.ds(0, ROWS_SETUP)], dom_in.at[slot_of(o)], peer(0, -o)) for o in pairs
        ] + [send(map_hbm, maps.at[1 + slot_of(o)], peer(0, -o)) for o in pairs]

    def send_close(target, k, outer):
        result = []
        for o in (k, -k):
            cols = pl.ds(512 * ((o > 0) == outer), 512)
            result.append(send(clo_hbm.at[:, cols], close.at[target, :, cols], peer(0, -o)))
        return result

    copies_first = send_state(1)
    copies_second = (
        send_state(2) + send_close(G1, 1, False) + send_state(3) + send_close(G2, 2, False)
    )

    own_pos = [state[pl.ds(8 * k, 8), :] for k in range(3)]
    centres = [jnp.mean(rows, axis=1, keepdims=True) for rows in own_pos]
    one = jnp.ones((8, LANES), F32)
    zero = jnp.zeros((8, LANES), F32)

    def put_features(rows_of, target, at):
        pos = [rows_of(k) - centres[k] for k in range(3)]
        line = [rows_of(3 + k) for k in range(3)]
        burg = [rows_of(6 + k) for k in range(3)]
        square = pos[0] * pos[0] + pos[1] * pos[1] + pos[2] * pos[2]
        products = [b * l for b in burg for l in line]
        if target:
            rest = [-2.0 * p for p in pos] + [square, one, zero, zero]
        else:
            rest = pos + [one, square + LONG_CORE * LONG_CORE, zero, zero]
            for k in range(3):
                feat_pos[at, pl.ds(8 * k, 8), :] = pos[k]
        for f, value in enumerate(products + rest):
            for piece, part in enumerate(split3(value)):
                feat[at, pl.ds((piece * 16 + f) * 8, 8), :] = part

    put_features(lambda k: state[pl.ds(8 * k, 8), :], True, 0)
    numerator_row = lax.broadcasted_iota(jnp.int32, (16, LANES), 0) < 9

    def build(q, carry):
        part = [feat[0, pl.ds(piece * 128 + q, 16, stride=8), :] for piece in range(3)]
        for half in range(2):
            keep = numerator_row if half == 0 else jnp.logical_not(numerator_row)
            rows = jnp.concatenate(
                [jnp.where(keep, part[i], 0.0) for i in (0, 0, 1, 0, 1, 2)]
                + [jnp.zeros((32, LANES), F32)],
                axis=0,
            )
            turned = rows.T.astype(BF16)
            for part_at in range(PARTS):
                lhs[q, pl.ds((2 * part_at + half) * PART, PART), :] = turned[
                    part_at * PART : (part_at + 1) * PART
                ]
        return carry

    lax.fori_loop(0, CELLS, build, 0)

    def long_blocks(count, first):
        def cell(q, carry):
            rhs = []
            for s in range(count):
                part = [feat[s, pl.ds(piece * 128 + q, 16, stride=8), :] for piece in range(3)]
                rhs.append(
                    jnp.concatenate(
                        [part[i] for i in (0, 1, 0, 2, 1, 0)] + [jnp.zeros((32, LANES), F32)],
                        axis=0,
                    ).astype(BF16)
                )
            for part_at in range(PARTS):
                rows = pl.ds(part_at * PART, PART)
                total = None if first else [acc[q, k, rows, :] for k in range(4)]
                for s in range(count):
                    both = jnp.dot(
                        lhs[q, pl.ds(2 * part_at * PART, 2 * PART), :],
                        rhs[s],
                        preferred_element_type=F32,
                    )
                    inverse = lax.rsqrt(both[PART:])
                    w = both[:PART] * inverse * (inverse * inverse)
                    terms = [w * feat_pos[s, pl.ds(8 * k + q, 1), :] for k in range(3)] + [w]
                    total = terms if total is None else [a + b for a, b in zip(total, terms)]
                for k in range(4):
                    acc[q, k, rows, :] = total[k]
            return carry

        lax.fori_loop(0, CELLS, cell, 0, unroll=2)

    put_features(lambda k: state[pl.ds(8 * k, 8), :], False, 0)
    long_blocks(1, True)
    row = lax.broadcasted_iota(jnp.int32, (8, LANES), 0)
    low_half = row < 4

    def merge(source, rows, k, outer):
        above, below = source[slot_of(k), rows, :], source[slot_of(-k), rows, :]
        if outer:
            return jnp.where(low_half, below, above)
        return jnp.where(low_half, above, below)

    near = {G1: (1, False), G2: (2, False), H1: (1, True), G3: (3, False), G4: (4, False), H2: (2, True)}

    def merge_into(target, first, source, source_first, components, groups):
        for g in groups:
            k, outer = near[g]
            for c in range(components):
                target[g, pl.ds(first + 8 * c, 8), :] = merge(
                    source, pl.ds(source_first + 8 * c, 8), k, outer
                )

    def put_maps(slots):
        for slot in slots:
            for j in range(4):
                map_all[pl.ds((slot * 4 + j) * SUBS, SUBS), :] = maps[
                    slot, :, pl.ds(j * LANES, LANES)
                ]

    def pick_windows(t, n_domains, n_groups, tile_of, target, start=0):
        for domain in DOMAINS[start:n_domains]:
            for g, first, slot, tile, served in windows_of(domain):
                place = map_all[pl.ds((slot * 4 + tile) * SUBS + t, 1), :]
                place = jnp.broadcast_to(place, (8, LANES))
                lane = place & 127
                at = (place >> 7) & 3
                picked = [take_lanes(tile_of(g, first + i), lane) for i in range(4)]
                odd = (at & 1) != 0
                result = jnp.where(
                    at >= 2,
                    jnp.where(odd, picked[3], picked[2]),
                    jnp.where(odd, picked[1], picked[0]),
                )
                for g_to, cell in served:
                    if g_to < n_groups:
                        target[pl.ds((g_to * 8 + cell) * 8, 8), :] = result

    def spread(value):
        return jnp.broadcast_to(value, (8, LANES))

    def close_of(g, s, r):
        return close[g, pl.ds(8 * r, 8), pl.ds(s * LANES, LANES)]

    def dots(mine, other):
        line = mine[0] * other[0] + mine[1] * other[1] + mine[2] * other[2]
        burg = mine[3] * other[3] + mine[4] * other[4] + mine[5] * other[5]
        return line * burg

    def static_rows(g, s):
        return [spread(group[g, pl.ds(24 + 8 * k + s, 1), :]) for k in range(6)]

    def weights_own(g, carry):
        for s in range(CELLS):
            mine = static_rows(g, s)
            for r in range(4):
                index = close_of(g, s, r)
                lane = index & 127
                other = [take_lanes(m, lane) for m in mine]
                weight_own[g, s, pl.ds(8 * r, 8), :] = jnp.where(
                    index < LANES, dots(mine, other), 0.0
                )
        return carry

    def static_tile(g, s):
        return group[g, pl.ds(24 + s, 8, stride=8), :]

    def weights_ghost(t, n_groups, start=0):
        pick_windows(t, DOMAINS_FOR[n_groups], n_groups, static_tile, statics_gh, start)

        def one(g, carry):
            for s in range(CELLS):
                mine = static_rows(g, s)
                base = (g * 8 + s) * 8
                theirs = [spread(statics_gh[pl.ds(base + k, 1), :]) for k in range(6)]
                for r in range(4):
                    index = close_of(g, s, r)
                    lane = index & 127
                    other = [take_lanes(m, lane) for m in theirs]
                    value = jnp.where(index < 2 * LANES, dots(mine, other), 0.0)
                    rows = pl.ds(8 * r, 8)
                    weight[t, g, s, rows, :] = jnp.where(
                        index < LANES, weight_own[g, s, rows, :], value
                    )
            return carry

        lax.fori_loop(start, n_groups, one, 0)

    short_scale = 1.0 / math.sqrt(SLOTS)

    def tiles_in(positions):
        return lambda g, s: positions[g, pl.ds(s, 8, stride=8), :]

    def evaluate(t, n_groups, positions):
        pick_windows(t, DOMAINS_FOR[n_groups], n_groups, tiles_in(positions), ghost)

        def one(g, carry):
            sums = [[], [], []]
            for s in range(CELLS):
                mine = [spread(positions[g, pl.ds(8 * k + s, 1), :]) for k in range(3)]
                base = (g * 8 + s) * 8
                theirs = [spread(ghost[pl.ds(base + k, 1), :]) for k in range(3)]
                total = None
                for r in range(4):
                    index = close_of(g, s, r)
                    lane = index & 127
                    is_ghost = index >= LANES
                    inner = [take_lanes(m, lane) for m in mine]
                    outer = [take_lanes(m, lane) for m in theirs]
                    delta = [
                        m - jnp.where(is_ghost, o, i) for m, o, i in zip(mine, outer, inner)
                    ]
                    radius = (
                        delta[0] * delta[0]
                        + delta[1] * delta[1]
                        + delta[2] * delta[2]
                        + SHORT_CORE * SHORT_CORE
                    )
                    inverse = lax.rsqrt(radius)
                    w = weight[t, g, s, pl.ds(8 * r, 8), :] * inverse * (inverse * inverse)
                    terms = [w * d for d in delta]
                    total = terms if total is None else [a + b for a, b in zip(total, terms)]
                for k in range(3):
                    sums[k].append(total[k])
            for k in range(3):
                frow[g, pl.ds(8 * k, 8), :] = fold_cells(sums[k], row)
            return carry

        lax.fori_loop(0, n_groups, one, 0)

    def drift(g, k):
        rows = pl.ds(8 * k, 8)
        force = group[g, pl.ds(ROW_F + 8 * k, 8), :] + frow[g, rows, :] * short_scale
        return group[g, pl.ds(ROW_MOB, 8), :] * force

    def make_guess(n_groups):
        for g in range(n_groups):
            for k in range(3):
                rows = pl.ds(8 * k, 8)
                first = drift(g, k)
                position = xnow[g, rows, :]
                vfirst[g, rows, :] = first
                xguess[g, rows, :] = position + STEP * first
                xhalf[g, rows, :] = position + (0.5 * STEP) * first

    def advance(n_groups):
        for g in range(n_groups):
            for k in range(3):
                rows = pl.ds(8 * k, 8)
                xnow[g, rows, :] = xhalf[g, rows, :] + (0.5 * STEP) * drift(g, k)

    for copy in local[4:]:
        copy.wait()
    lax.fori_loop(0, 1, weights_own, 0)
    put_maps((0,))
    for i in range(4):
        blk_copies[i].wait_recv()
        put_features(lambda k: far_blk[i, pl.ds(8 * k, 8), :], False, i)
    long_blocks(4, False)

    lane_id = lax.broadcasted_iota(jnp.int32, (LANES, LANES), 1)

    def reduce_cell(q, columns):
        for k in range(4):
            total = jnp.sum(acc[q, k], axis=1, keepdims=True)
            columns = jnp.where(lane_id == k * 8 + q, total, columns)
        return columns

    columns = lax.fori_loop(
        0, CELLS, reduce_cell, jnp.zeros((LANES, LANES), F32), unroll=4
    )
    sums = columns.T
    scale = 1.0 / math.sqrt(5 * LANES)
    for k in range(3):
        force = ((own_pos[k] - centres[k]) * sums[24:32] - sums[8 * k : 8 * k + 8]) * scale
        state[pl.ds(ROW_F + 8 * k, 8), :] = force


    for copy in copies_first:
        copy.wait_recv()
    merge_into(group, 0, dom_in, 0, 10, (G1, H1))
    put_maps((1, 2))
    xnow[G0, pl.ds(0, 24), :] = state[pl.ds(0, 24), :]
    xnow[G1, pl.ds(0, 24), :] = group[G1, pl.ds(0, 24), :]
    weights_ghost(0, 1)
    evaluate(0, 1, xnow)
    make_guess(1)
    for k in range(3):
        for part, ref in ((0, xguess), (24, xhalf)):
            msend[pl.ds(part + 8 * k, 8), :] = ref[G0, pl.ds(8 * k, 8), :]
        msend[pl.ds(48 + 8 * k, 8), :] = group[G0, pl.ds(ROW_F + 8 * k, 8), :]
    m_copies = [send(msend, mrecv.at[slot_of(o)], peer(0, -o)) for o in OFFSETS[:6]]
    copies_third = send_close(H1, 1, True) + send_close(G3, 3, False) + send_state(4)

    for copy in copies_second:
        copy.wait_recv()
    merge_into(group, 0, dom_in, 0, 10, (G2, G3, H2))
    put_maps((3, 4, 5, 6))
    lax.fori_loop(1, 3, weights_own, 0)
    weights_ghost(0, 3, 1)
    weights_ghost(1, 2)
    for copy in m_copies:
        copy.wait_recv()
    merge_into(xguess, 0, mrecv, 0, 3, (G1, G2, H1, G3))
    merge_into(xhalf, 0, mrecv, 24, 3, (G1, G2))
    merge_into(group, ROW_F, mrecv, 48, 3, (G1, G2, H1, G3))
    evaluate(0, 3, xguess)
    advance(3)
    evaluate(1, 2, xnow)
    make_guess(2)
    evaluate(1, 1, xguess)
    advance(1)
    xsend[...] = xnow[G0, pl.ds(0, 24), :]
    x_copies = [send(xsend, xrecv.at[slot_of(o)], peer(0, -o)) for o in OFFSETS]

    for copy in copies_third:
        copy.wait_recv()
    merge_into(group, 0, dom_in, 0, 10, (G4,))
    put_maps((7, 8))
    lax.fori_loop(3, 5, weights_own, 0)
    weights_ghost(2, 5)
    weights_ghost(3, 2)
    for copy in x_copies:
        copy.wait_recv()
    merge_into(xnow, 0, xrecv, 0, 3, (G1, G2, H1, G3, G4, H2))
    evaluate(2, 5, xnow)
    make_guess(5)
    evaluate(2, 3, xguess)
    advance(3)
    evaluate(3, 2, xnow)
    make_guess(2)
    evaluate(3, 1, xguess)
    for k in range(3):
        twice = vfirst[G0, pl.ds(8 * k, 8), :] + drift(G0, k)
        position = xnow[G0, pl.ds(8 * k, 8), :]
        for q in range(CELLS):
            cols = pl.ds(q * LANES, LANES)
            pos_out[pl.ds(k, 1), cols] = position[q : q + 1, :]
            vel_out[pl.ds(k, 1), cols] = twice[q : q + 1, :]

    for copy in sends:
        copy.wait_send()


def solution(mesh):
    n_blk, n_dom = mesh.shape["blk"], mesh.shape["dom"]

    def step(positions, line_vectors, burgers, mobility, close_list, ghost_map):
        count = positions.shape[1]
        anywhere = pl.BlockSpec(memory_space=pl.ANY)
        vmem = pl.BlockSpec(memory_space=pltpu.VMEM)
        shape = jax.ShapeDtypeStruct((3, count), F32)
        n_sends = 4 + 8 + 8 + 8 + 6 + 8
        base, twice = pl.pallas_call(
            functools.partial(kernel, n_blk, n_dom),
            out_shape=(shape, shape),
            in_specs=[anywhere] * 6,
            out_specs=(vmem, vmem),
            scratch_shapes=[
                pltpu.VMEM((3, count), F32),
                pltpu.VMEM((3, count), F32),
                pltpu.VMEM((3, count), F32),
                pltpu.VMEM((1, count), F32),
                pltpu.VMEM((4, 72, LANES), F32),
                pltpu.VMEM((8, ROWS_SETUP, LANES), F32),
                pltpu.VMEM((7, ROWS_ALL, LANES), F32),
                pltpu.VMEM((5, SLOTS, count), jnp.int32),
                pltpu.VMEM((9, SUBS, 512), jnp.int32),
                pltpu.VMEM((144, LANES), jnp.int32),
                pltpu.VMEM((4, 384, LANES), F32),
                pltpu.VMEM((4, 24, LANES), F32),
                pltpu.VMEM((CELLS, 256, LANES), BF16),
                pltpu.VMEM((CELLS, 4, LANES, LANES), F32),
                pltpu.VMEM((320, LANES), F32),
                pltpu.VMEM((5, CELLS, SLOTS, LANES), F32),
                pltpu.VMEM((SUBS, 5, CELLS, SLOTS, LANES), F32),
                pltpu.VMEM((320, LANES), F32),
                pltpu.VMEM((5, 24, LANES), F32),
                pltpu.VMEM((5, 24, LANES), F32),
                pltpu.VMEM((7, 64, LANES), F32),
                pltpu.VMEM((5, 64, LANES), F32),
                pltpu.VMEM((5, 24, LANES), F32),
                pltpu.VMEM((72, LANES), F32),
                pltpu.VMEM((6, 72, LANES), F32),
                pltpu.VMEM((24, LANES), F32),
                pltpu.VMEM((8, 24, LANES), F32),
                pltpu.SemaphoreType.DMA((6,)),
                pltpu.SemaphoreType.DMA((n_sends,)),
                pltpu.SemaphoreType.DMA((n_sends,)),
            ],
            compiler_params=pltpu.CompilerParams(collective_id=0, has_side_effects=True),
        )(positions, line_vectors, burgers, mobility.reshape(1, count), close_list, ghost_map)
        return base + (0.5 * STEP) * twice, 0.5 * twice

    both = ("blk", "dom")
    return jax.shard_map(
        step,
        mesh=mesh,
        in_specs=(
            P(None, both),
            P(None, both),
            P(None, both),
            P(both),
            P(None, both),
            P(None, both),
        ),
        out_specs=(P(None, both), P(None, both)),
        check_vma=False,
    )
```

```python
import functools
import math

import jax
import jax.numpy as jnp
from jax import lax
from jax.experimental import pallas as pl
from jax.experimental.pallas import tpu as pltpu
from jax.sharding import PartitionSpec as P

MESH = pl.DeviceIdType.MESH
F32 = jnp.float32
BF16 = jnp.bfloat16

LANES = 128
CELLS = 8
PARTS = 4
PART = 32
SLOTS = 32
SUBS = 4
LONG_CORE = 1.0
SHORT_CORE = 0.25
STEP = 0.05

ROWS_SETUP = 80
ROW_MOB = 72
ROW_F = 80
ROWS_ALL = 112

REACH = 4
OFFSETS = tuple(sign * k for k in range(1, REACH + 1) for sign in (1, -1))
BLK_STEPS = (1, -1, 2, -2)

G0, G1, G2, H1, G3, G4, H2 = range(7)
GROUPS_NEAR = {1: G1, 2: G2, 3: G3, 4: G4}
GROUPS_OUTER = {1: H1, 2: H2}
DOMAINS_FOR = {1: 1, 2: 3, 3: 5, 5: 7}
DOMAINS = (0, 1, -1, 2, -2, 3, -3)


def slot_of(offset):
    return 2 * (abs(offset) - 1) + (offset < 0)


def upper_half(domain):
    if domain == 0:
        return G0
    return GROUPS_OUTER[domain] if domain > 0 else GROUPS_NEAR[-domain]


def lower_half(domain):
    if domain == 0:
        return G0
    return GROUPS_NEAR[domain] if domain > 0 else GROUPS_OUTER[-domain]


def windows_of(domain):
    result = []
    for w in range(4):
        near = domain - 1 if w < 2 else domain + 1
        group = upper_half(near) if w < 2 else lower_half(near)
        first = 4 if w < 2 else 0
        slot = 0 if near == 0 else 1 + slot_of(near)
        tile = 2 + w if w < 2 else w - 2
        served = []
        for half, cell in ((lower_half, w), (upper_half, 4 + w)):
            if abs(domain) in (0, 1) or half is (lower_half if domain > 0 else upper_half):
                served.append((half(domain), cell))
        result.append((group, first, slot, tile, served))
    return result


GATHER = lax.GatherDimensionNumbers(
    offset_dims=(),
    collapsed_slice_dims=(1,),
    start_index_map=(1,),
    operand_batching_dims=(0,),
    start_indices_batching_dims=(0,),
)


def take_lanes(rows, lane):
    return lax.gather(
        rows,
        lane[..., None],
        GATHER,
        slice_sizes=(1, 1),
        mode=lax.GatherScatterMode.PROMISE_IN_BOUNDS,
    )


def split3(value):
    high = value.astype(BF16)
    rest = value - high.astype(F32)
    mid = rest.astype(BF16)
    low = (rest - mid.astype(F32)).astype(BF16)
    return high.astype(F32), mid.astype(F32), low.astype(F32)


def fold_cells(parts, row):
    def join(a, b, mask, turn):
        return jnp.where(mask, a, b) + pltpu.roll(jnp.where(mask, b, a), turn, 0)

    def turned(start):
        return jnp.bitwise_and(row - start, 7)

    pairs = [join(parts[s], parts[s + 4], turned(s) < 4, 4) for s in range(4)]
    quads = [
        join(pairs[s], pairs[s + 2], jnp.bitwise_and(turned(s), 2) == 0, 6) for s in range(2)
    ]
    return join(quads[0], quads[1], jnp.bitwise_and(row, 1) == 0, 7)


def kernel(
    n_blk,
    n_dom,
    pos_hbm,
    lin_hbm,
    bur_hbm,
    mob_hbm,
    clo_hbm,
    map_hbm,
    pos_out,
    vel_out,
    pos_v,
    lin_v,
    bur_v,
    mob_v,
    far_blk,
    dom_in,
    group,
    close,
    maps,
    map_all,
    feat,
    feat_pos,
    lhs,
    acc,
    statics_gh,
    weight_own,
    weight,
    ghost,
    frow,
    vfirst,
    xnow,
    xguess,
    xhalf,
    msend,
    mrecv,
    xsend,
    xrecv,
    local_sem,
    send_sem,
    recv_sem,
):
    me_b = lax.axis_index("blk")
    me_d = lax.axis_index("dom")

    def peer(db, dd):
        return {
            "blk": lax.rem(me_b + db + n_blk, n_blk),
            "dom": lax.rem(me_d + dd + n_dom, n_dom),
        }

    local = []
    for i, (src, dst) in enumerate(
        (
            (pos_hbm, pos_v),
            (lin_hbm, lin_v),
            (bur_hbm, bur_v),
            (mob_hbm, mob_v),
            (clo_hbm, close.at[G0]),
            (map_hbm, maps.at[0]),
        )
    ):
        copy = pltpu.make_async_copy(src, dst, local_sem.at[i])
        copy.start()
        local.append(copy)

    barrier = pltpu.get_barrier_semaphore()
    for step in BLK_STEPS:
        pl.semaphore_signal(barrier, inc=1, device_id=peer(step, 0), device_id_type=MESH)
    for step in OFFSETS:
        pl.semaphore_signal(barrier, inc=1, device_id=peer(0, step), device_id_type=MESH)

    for copy in local[:4]:
        copy.wait()
    state = group.at[G0]
    for first, ref in ((0, pos_v), (24, lin_v), (48, bur_v), (72, mob_v)):
        for k in range(ref.shape[0]):
            for q in range(CELLS):
                state[pl.ds(first + k * 8 + q, 1), :] = ref[pl.ds(k, 1), pl.ds(q * LANES, LANES)]

    pl.semaphore_wait(barrier, len(BLK_STEPS) + len(OFFSETS))

    sends = []

    def send(src, dst, device):
        i = len(sends)
        copy = pltpu.make_async_remote_copy(
            src_ref=src,
            dst_ref=dst,
            send_sem=send_sem.at[i],
            recv_sem=recv_sem.at[i],
            device_id=device,
            device_id_type=MESH,
        )
        copy.start()
        sends.append(copy)
        return copy

    blk_copies = [
        send(state.at[pl.ds(0, 72)], far_blk.at[i], peer(step, 0))
        for i, step in enumerate(BLK_STEPS)
    ]

    def landing(o, outer):
        return 8 + (o < 0) if outer else slot_of(o)

    def halves(ref, components, half):
        view = ref.reshape(ref.shape[0] // 8, 8, LANES)
        return view.at[components, pl.ds(4 * half, 4), :]

    def send_maps(k, outer):
        result = []
        for o in (k, -k):
            cols = pl.ds(256 * ((o > 0) == outer), 256)
            result.append(
                send(map_hbm.at[:, cols], maps.at[1 + landing(o, outer), :, cols], peer(0, -o))
            )
        return result

    def send_statics(k, outer):
        result = []
        for o in (k, -k):
            half = (o > 0) == outer
            result.append(
                send(
                    halves(state, pl.ds(3, 7), half),
                    halves(dom_in.at[landing(o, outer)], pl.ds(3, 7), half),
                    peer(0, -o),
                )
            )
        return result

    def send_first(k):
        pairs = (k, -k)
        return [
            send(state.at[pl.ds(0, ROWS_SETUP)], dom_in.at[slot_of(o)], peer(0, -o)) for o in pairs
        ] + [send(map_hbm, maps.at[1 + slot_of(o)], peer(0, -o)) for o in pairs]

    def send_close(target, k, outer):
        result = []
        for o in (k, -k):
            cols = pl.ds(512 * ((o > 0) == outer), 512)
            result.append(send(clo_hbm.at[:, cols], close.at[target, :, cols], peer(0, -o)))
        return result

    copies_first = send_first(1)
    copies_second = (
        send_close(G1, 1, False)
        + send_statics(2, False)
        + send_maps(2, False)
        + send_statics(3, False)
        + send_maps(3, False)
        + send_close(G2, 2, False)
    )

    own_pos = [state[pl.ds(8 * k, 8), :] for k in range(3)]
    centres = [jnp.mean(rows, axis=1, keepdims=True) for rows in own_pos]
    one = jnp.ones((8, LANES), F32)
    zero = jnp.zeros((8, LANES), F32)

    def put_features(rows_of, target, at):
        pos = [rows_of(k) - centres[k] for k in range(3)]
        line = [rows_of(3 + k) for k in range(3)]
        burg = [rows_of(6 + k) for k in range(3)]
        square = pos[0] * pos[0] + pos[1] * pos[1] + pos[2] * pos[2]
        products = [b * l for b in burg for l in line]
        if target:
            rest = [-2.0 * p for p in pos] + [square, one, zero, zero]
        else:
            rest = pos + [one, square + LONG_CORE * LONG_CORE, zero, zero]
            for k in range(3):
                feat_pos[at, pl.ds(8 * k, 8), :] = pos[k]
        for f, value in enumerate(products + rest):
            for piece, part in enumerate(split3(value)):
                feat[at, pl.ds((piece * 16 + f) * 8, 8), :] = part

    put_features(lambda k: state[pl.ds(8 * k, 8), :], True, 0)
    numerator_row = lax.broadcasted_iota(jnp.int32, (16, LANES), 0) < 9

    def build(q, carry):
        part = [feat[0, pl.ds(piece * 128 + q, 16, stride=8), :] for piece in range(3)]
        for half in range(2):
            keep = numerator_row if half == 0 else jnp.logical_not(numerator_row)
            rows = jnp.concatenate(
                [jnp.where(keep, part[i], 0.0) for i in (0, 0, 1, 0, 1, 2)]
                + [jnp.zeros((32, LANES), F32)],
                axis=0,
            )
            turned = rows.T.astype(BF16)
            for part_at in range(PARTS):
                lhs[q, pl.ds((2 * part_at + half) * PART, PART), :] = turned[
                    part_at * PART : (part_at + 1) * PART
                ]
        return carry

    lax.fori_loop(0, CELLS, build, 0)

    def long_blocks(count, first):
        def cell(q, carry):
            rhs = []
            for s in range(count):
                part = [feat[s, pl.ds(piece * 128 + q, 16, stride=8), :] for piece in range(3)]
                rhs.append(
                    jnp.concatenate(
                        [part[i] for i in (0, 1, 0, 2, 1, 0)] + [jnp.zeros((32, LANES), F32)],
                        axis=0,
                    ).astype(BF16)
                )
            for part_at in range(PARTS):
                rows = pl.ds(part_at * PART, PART)
                total = None if first else [acc[q, k, rows, :] for k in range(4)]
                for s in range(count):
                    both = jnp.dot(
                        lhs[q, pl.ds(2 * part_at * PART, 2 * PART), :],
                        rhs[s],
                        preferred_element_type=F32,
                    )
                    inverse = lax.rsqrt(both[PART:])
                    w = both[:PART] * inverse * (inverse * inverse)
                    terms = [w * feat_pos[s, pl.ds(8 * k + q, 1), :] for k in range(3)] + [w]
                    total = terms if total is None else [a + b for a, b in zip(total, terms)]
                for k in range(4):
                    acc[q, k, rows, :] = total[k]
            return carry

        lax.fori_loop(0, CELLS, cell, 0, unroll=4)

    put_features(lambda k: state[pl.ds(8 * k, 8), :], False, 0)
    long_blocks(1, True)
    row = lax.broadcasted_iota(jnp.int32, (8, LANES), 0)
    low_half = row < 4

    def merge(source, rows, k, outer, first=None):
        first = slot_of(k) if first is None else first
        above, below = source[first, rows, :], source[first + 1, rows, :]
        if outer:
            return jnp.where(low_half, below, above)
        return jnp.where(low_half, above, below)

    near = {G1: (1, False), G2: (2, False), H1: (1, True), G3: (3, False), G4: (4, False), H2: (2, True)}

    def merge_into(target, first, source, source_first, components, groups, slot=None):
        for g in groups:
            k, outer = near[g]
            for c in range(components):
                target[g, pl.ds(first + 8 * c, 8), :] = merge(
                    source, pl.ds(source_first + 8 * c, 8), k, outer, slot
                )

    def put_maps(source, slot, tiles):
        for j in tiles:
            map_all[pl.ds((slot * 4 + j) * SUBS, SUBS), :] = maps[
                source, :, pl.ds(j * LANES, LANES)
            ]

    def put_near_maps(k):
        put_maps(1 + slot_of(k), 1 + slot_of(k), (0, 1))
        put_maps(1 + slot_of(-k), 1 + slot_of(-k), (2, 3))

    def pick_windows(t, n_domains, n_groups, tile_of, target, start=0):
        for domain in DOMAINS[start:n_domains]:
            for g, first, slot, tile, served in windows_of(domain):
                place = map_all[pl.ds((slot * 4 + tile) * SUBS + t, 1), :]
                place = jnp.broadcast_to(place, (8, LANES))
                lane = place & 127
                at = (place >> 7) & 3
                picked = [take_lanes(tile_of(g, first + i), lane) for i in range(4)]
                odd = (at & 1) != 0
                result = jnp.where(
                    at >= 2,
                    jnp.where(odd, picked[3], picked[2]),
                    jnp.where(odd, picked[1], picked[0]),
                )
                for g_to, cell in served:
                    if g_to < n_groups:
                        target[pl.ds((g_to * 8 + cell) * 8, 8), :] = result

    def spread(value):
        return jnp.broadcast_to(value, (8, LANES))

    def close_of(g, s, r):
        return close[g, pl.ds(8 * r, 8), pl.ds(s * LANES, LANES)]

    def dots(mine, other):
        line = mine[0] * other[0] + mine[1] * other[1] + mine[2] * other[2]
        burg = mine[3] * other[3] + mine[4] * other[4] + mine[5] * other[5]
        return line * burg

    def static_rows(g, s):
        return [spread(group[g, pl.ds(24 + 8 * k + s, 1), :]) for k in range(6)]

    def weights_own(g, carry):
        for s in range(CELLS):
            mine = static_rows(g, s)
            for r in range(4):
                index = close_of(g, s, r)
                lane = index & 127
                other = [take_lanes(m, lane) for m in mine]
                weight_own[g, s, pl.ds(8 * r, 8), :] = jnp.where(
                    index < LANES, dots(mine, other), 0.0
                )
        return carry

    def static_tile(g, s):
        return group[g, pl.ds(24 + s, 8, stride=8), :]

    def weights_ghost(t, n_groups, start=0):
        pick_windows(t, DOMAINS_FOR[n_groups], n_groups, static_tile, statics_gh, start)

        def one(g, carry):
            for s in range(CELLS):
                mine = static_rows(g, s)
                base = (g * 8 + s) * 8
                theirs = [spread(statics_gh[pl.ds(base + k, 1), :]) for k in range(6)]
                for r in range(4):
                    index = close_of(g, s, r)
                    lane = index & 127
                    other = [take_lanes(m, lane) for m in theirs]
                    value = jnp.where(index < 2 * LANES, dots(mine, other), 0.0)
                    rows = pl.ds(8 * r, 8)
                    weight[t, g, s, rows, :] = jnp.where(
                        index < LANES, weight_own[g, s, rows, :], value
                    )
            return carry

        lax.fori_loop(start, n_groups, one, 0)

    short_scale = 1.0 / math.sqrt(SLOTS)

    def tiles_in(positions):
        return lambda g, s: positions[g, pl.ds(s, 8, stride=8), :]

    def evaluate(t, n_groups, positions):
        pick_windows(t, DOMAINS_FOR[n_groups], n_groups, tiles_in(positions), ghost)

        def one(g, carry):
            sums = [[], [], []]
            for s in range(CELLS):
                mine = [spread(positions[g, pl.ds(8 * k + s, 1), :]) for k in range(3)]
                base = (g * 8 + s) * 8
                theirs = [spread(ghost[pl.ds(base + k, 1), :]) for k in range(3)]
                total = None
                for r in range(4):
                    index = close_of(g, s, r)
                    lane = index & 127
                    is_ghost = index >= LANES
                    inner = [take_lanes(m, lane) for m in mine]
                    outer = [take_lanes(m, lane) for m in theirs]
                    delta = [
                        m - jnp.where(is_ghost, o, i) for m, o, i in zip(mine, outer, inner)
                    ]
                    radius = (
                        delta[0] * delta[0]
                        + delta[1] * delta[1]
                        + delta[2] * delta[2]
                        + SHORT_CORE * SHORT_CORE
                    )
                    inverse = lax.rsqrt(radius)
                    w = weight[t, g, s, pl.ds(8 * r, 8), :] * inverse * (inverse * inverse)
                    terms = [w * d for d in delta]
                    total = terms if total is None else [a + b for a, b in zip(total, terms)]
                for k in range(3):
                    sums[k].append(total[k])
            for k in range(3):
                frow[g, pl.ds(8 * k, 8), :] = fold_cells(sums[k], row)
            return carry

        lax.fori_loop(0, n_groups, one, 0)

    def drift(g, k):
        rows = pl.ds(8 * k, 8)
        force = group[g, pl.ds(ROW_F + 8 * k, 8), :] + frow[g, rows, :] * short_scale
        return group[g, pl.ds(ROW_MOB, 8), :] * force

    def make_guess(n_groups):
        for g in range(n_groups):
            for k in range(3):
                rows = pl.ds(8 * k, 8)
                first = drift(g, k)
                position = xnow[g, rows, :]
                vfirst[g, rows, :] = first
                xguess[g, rows, :] = position + STEP * first
                xhalf[g, rows, :] = position + (0.5 * STEP) * first

    def advance(n_groups):
        for g in range(n_groups):
            for k in range(3):
                rows = pl.ds(8 * k, 8)
                xnow[g, rows, :] = xhalf[g, rows, :] + (0.5 * STEP) * drift(g, k)

    for copy in local[4:]:
        copy.wait()
    lax.fori_loop(0, 1, weights_own, 0)
    put_maps(0, 0, range(4))
    for i in range(4):
        blk_copies[i].wait_recv()
        put_features(lambda k: far_blk[i, pl.ds(8 * k, 8), :], False, i)
    long_blocks(4, False)

    lane_id = lax.broadcasted_iota(jnp.int32, (LANES, LANES), 1)

    def reduce_cell(q, columns):
        for k in range(4):
            total = jnp.sum(acc[q, k], axis=1, keepdims=True)
            columns = jnp.where(lane_id == k * 8 + q, total, columns)
        return columns

    columns = lax.fori_loop(
        0, CELLS, reduce_cell, jnp.zeros((LANES, LANES), F32), unroll=8
    )
    sums = columns.T
    scale = 1.0 / math.sqrt(5 * LANES)
    for k in range(3):
        force = ((own_pos[k] - centres[k]) * sums[24:32] - sums[8 * k : 8 * k + 8]) * scale
        state[pl.ds(ROW_F + 8 * k, 8), :] = force


    for copy in copies_first:
        copy.wait_recv()
    merge_into(group, 0, dom_in, 0, 10, (G1, H1))
    put_maps(1, 1, range(4))
    put_maps(2, 2, range(4))
    xnow[G0, pl.ds(0, 24), :] = state[pl.ds(0, 24), :]
    xnow[G1, pl.ds(0, 24), :] = group[G1, pl.ds(0, 24), :]
    weights_ghost(0, 1)
    evaluate(0, 1, xnow)
    make_guess(1)
    for k in range(3):
        for part, ref in ((0, xguess), (48, xhalf)):
            msend[pl.ds(part + 8 * k, 8), :] = ref[G0, pl.ds(8 * k, 8), :]
        msend[pl.ds(24 + 8 * k, 8), :] = group[G0, pl.ds(ROW_F + 8 * k, 8), :]
    m_copies = [send(msend, mrecv.at[slot_of(o)], peer(0, -o)) for o in OFFSETS[:2]]
    for k, count in ((2, 9), (3, 6)):
        for o in (k, -k):
            part = functools.partial(halves, components=pl.ds(0, count), half=o < 0)
            m_copies.append(send(part(msend), part(mrecv.at[slot_of(o)]), peer(0, -o)))
    copies_third = (
        send_close(H1, 1, True)
        + send_close(G3, 3, False)
        + send_statics(2, True)
        + send_maps(2, True)
        + send_statics(4, False)
        + send_maps(4, False)
    )

    for copy in copies_second:
        copy.wait_recv()
    merge_into(group, 24, dom_in, 24, 7, (G2, G3))
    put_near_maps(2)
    put_near_maps(3)
    lax.fori_loop(1, 3, weights_own, 0)
    weights_ghost(0, 3, 1)
    weights_ghost(1, 2)
    for copy in m_copies:
        copy.wait_recv()
    merge_into(xguess, 0, mrecv, 0, 3, (G1, G2, H1, G3))
    merge_into(xhalf, 0, mrecv, 48, 3, (G1, G2))
    merge_into(group, ROW_F, mrecv, 24, 3, (G1, G2, H1, G3))
    evaluate(0, 3, xguess)
    advance(3)
    evaluate(1, 2, xnow)
    make_guess(2)
    evaluate(1, 1, xguess)
    advance(1)
    xsend[...] = xnow[G0, pl.ds(0, 24), :]
    x_copies = [send(xsend, xrecv.at[slot_of(o)], peer(0, -o)) for o in OFFSETS[:4]]
    for o in OFFSETS[4:]:
        part = functools.partial(halves, components=pl.ds(0, 3), half=o < 0)
        x_copies.append(send(part(xsend), part(xrecv.at[slot_of(o)]), peer(0, -o)))

    for copy in copies_third:
        copy.wait_recv()
    merge_into(group, 24, dom_in, 24, 7, (G4,))
    merge_into(group, 24, dom_in, 24, 7, (H2,), 8)
    put_near_maps(4)
    put_maps(9, 3, (2, 3))
    put_maps(10, 4, (0, 1))
    lax.fori_loop(3, 5, weights_own, 0)
    weights_ghost(2, 5)
    weights_ghost(3, 2)
    for copy in x_copies:
        copy.wait_recv()
    merge_into(xnow, 0, xrecv, 0, 3, (G1, G2, H1, G3, G4, H2))
    evaluate(2, 5, xnow)
    make_guess(5)
    evaluate(2, 3, xguess)
    advance(3)
    evaluate(3, 2, xnow)
    make_guess(2)
    evaluate(3, 1, xguess)
    for k in range(3):
        twice = vfirst[G0, pl.ds(8 * k, 8), :] + drift(G0, k)
        position = xnow[G0, pl.ds(8 * k, 8), :]
        for q in range(CELLS):
            cols = pl.ds(q * LANES, LANES)
            pos_out[pl.ds(k, 1), cols] = position[q : q + 1, :]
            vel_out[pl.ds(k, 1), cols] = twice[q : q + 1, :]

    for copy in sends:
        copy.wait_send()


def solution(mesh):
    n_blk, n_dom = mesh.shape["blk"], mesh.shape["dom"]

    def step(positions, line_vectors, burgers, mobility, close_list, ghost_map):
        count = positions.shape[1]
        anywhere = pl.BlockSpec(memory_space=pl.ANY)
        vmem = pl.BlockSpec(memory_space=pltpu.VMEM)
        shape = jax.ShapeDtypeStruct((3, count), F32)
        n_sends = 4 + 4 + 12 + 12 + 6 + 8
        base, twice = pl.pallas_call(
            functools.partial(kernel, n_blk, n_dom),
            out_shape=(shape, shape),
            in_specs=[anywhere] * 6,
            out_specs=(vmem, vmem),
            scratch_shapes=[
                pltpu.VMEM((3, count), F32),
                pltpu.VMEM((3, count), F32),
                pltpu.VMEM((3, count), F32),
                pltpu.VMEM((1, count), F32),
                pltpu.VMEM((4, 72, LANES), F32),
                pltpu.VMEM((10, ROWS_SETUP, LANES), F32),
                pltpu.VMEM((7, ROWS_ALL, LANES), F32),
                pltpu.VMEM((5, SLOTS, count), jnp.int32),
                pltpu.VMEM((11, SUBS, 512), jnp.int32),
                pltpu.VMEM((144, LANES), jnp.int32),
                pltpu.VMEM((4, 384, LANES), F32),
                pltpu.VMEM((4, 24, LANES), F32),
                pltpu.VMEM((CELLS, 256, LANES), BF16),
                pltpu.VMEM((CELLS, 4, LANES, LANES), F32),
                pltpu.VMEM((320, LANES), F32),
                pltpu.VMEM((5, CELLS, SLOTS, LANES), F32),
                pltpu.VMEM((SUBS, 5, CELLS, SLOTS, LANES), F32),
                pltpu.VMEM((320, LANES), F32),
                pltpu.VMEM((5, 24, LANES), F32),
                pltpu.VMEM((5, 24, LANES), F32),
                pltpu.VMEM((7, 64, LANES), F32),
                pltpu.VMEM((5, 64, LANES), F32),
                pltpu.VMEM((5, 24, LANES), F32),
                pltpu.VMEM((72, LANES), F32),
                pltpu.VMEM((6, 72, LANES), F32),
                pltpu.VMEM((24, LANES), F32),
                pltpu.VMEM((8, 24, LANES), F32),
                pltpu.SemaphoreType.DMA((6,)),
                pltpu.SemaphoreType.DMA((n_sends,)),
                pltpu.SemaphoreType.DMA((n_sends,)),
            ],
            compiler_params=pltpu.CompilerParams(collective_id=0, has_side_effects=True),
        )(positions, line_vectors, burgers, mobility.reshape(1, count), close_list, ghost_map)
        return base + (0.5 * STEP) * twice, 0.5 * twice

    both = ("blk", "dom")
    return jax.shard_map(
        step,
        mesh=mesh,
        in_specs=(
            P(None, both),
            P(None, both),
            P(None, both),
            P(both),
            P(None, both),
            P(None, both),
        ),
        out_specs=(P(None, both), P(None, both)),
        check_vma=False,
    )
```

```python
import functools
import math

import jax
import jax.numpy as jnp
from jax import lax
from jax.experimental import pallas as pl
from jax.experimental.pallas import tpu as pltpu
from jax.sharding import PartitionSpec as P

MESH = pl.DeviceIdType.MESH
F32 = jnp.float32
BF16 = jnp.bfloat16

LANES = 128
CELLS = 8
PARTS = 4
PART = 32
SLOTS = 32
SUBS = 4
LONG_CORE = 1.0
SHORT_CORE = 0.25
STEP = 0.05

ROWS_SETUP = 80
ROW_MOB = 72
ROW_F = 80
ROWS_ALL = 112

REACH = 4
OFFSETS = tuple(sign * k for k in range(1, REACH + 1) for sign in (1, -1))
BLK_STEPS = (1, -1, 2, -2)

G0, G1, G2, H1, G3, G4, H2 = range(7)
GROUPS_NEAR = {1: G1, 2: G2, 3: G3, 4: G4}
GROUPS_OUTER = {1: H1, 2: H2}
DOMAINS_FOR = {1: 1, 2: 3, 3: 5, 5: 7}
DOMAINS = (0, 1, -1, 2, -2, 3, -3)


def slot_of(offset):
    return 2 * (abs(offset) - 1) + (offset < 0)


def upper_half(domain):
    if domain == 0:
        return G0
    return GROUPS_OUTER[domain] if domain > 0 else GROUPS_NEAR[-domain]


def lower_half(domain):
    if domain == 0:
        return G0
    return GROUPS_NEAR[domain] if domain > 0 else GROUPS_OUTER[-domain]


def windows_of(domain):
    result = []
    for w in range(4):
        near = domain - 1 if w < 2 else domain + 1
        group = upper_half(near) if w < 2 else lower_half(near)
        first = 4 if w < 2 else 0
        slot = 0 if near == 0 else 1 + slot_of(near)
        tile = 2 + w if w < 2 else w - 2
        served = []
        for half, cell in ((lower_half, w), (upper_half, 4 + w)):
            if abs(domain) in (0, 1) or half is (lower_half if domain > 0 else upper_half):
                served.append((half(domain), cell))
        result.append((group, first, slot, tile, served))
    return result


GATHER = lax.GatherDimensionNumbers(
    offset_dims=(),
    collapsed_slice_dims=(1,),
    start_index_map=(1,),
    operand_batching_dims=(0,),
    start_indices_batching_dims=(0,),
)


def take_lanes(rows, lane):
    return lax.gather(
        rows,
        lane[..., None],
        GATHER,
        slice_sizes=(1, 1),
        mode=lax.GatherScatterMode.PROMISE_IN_BOUNDS,
    )


def split3(value):
    high = value.astype(BF16)
    rest = value - high.astype(F32)
    mid = rest.astype(BF16)
    low = (rest - mid.astype(F32)).astype(BF16)
    return high.astype(F32), mid.astype(F32), low.astype(F32)


def fold_cells(parts, row):
    def join(a, b, mask, turn):
        return jnp.where(mask, a, b) + pltpu.roll(jnp.where(mask, b, a), turn, 0)

    def turned(start):
        return jnp.bitwise_and(row - start, 7)

    pairs = [join(parts[s], parts[s + 4], turned(s) < 4, 4) for s in range(4)]
    quads = [
        join(pairs[s], pairs[s + 2], jnp.bitwise_and(turned(s), 2) == 0, 6) for s in range(2)
    ]
    return join(quads[0], quads[1], jnp.bitwise_and(row, 1) == 0, 7)


def kernel(
    n_blk,
    n_dom,
    pos_hbm,
    lin_hbm,
    bur_hbm,
    mob_hbm,
    clo_hbm,
    map_hbm,
    pos_out,
    vel_out,
    pos_v,
    lin_v,
    bur_v,
    mob_v,
    far_blk,
    dom_in,
    group,
    close,
    maps,
    map_all,
    feat,
    feat_pos,
    lhs,
    acc,
    statics_gh,
    weight_own,
    weight,
    ghost,
    frow,
    vfirst,
    xnow,
    xguess,
    xhalf,
    msend,
    mrecv,
    xsend,
    xrecv,
    local_sem,
    send_sem,
    recv_sem,
):
    me_b = lax.axis_index("blk")
    me_d = lax.axis_index("dom")

    def peer(db, dd):
        return {
            "blk": lax.rem(me_b + db + n_blk, n_blk),
            "dom": lax.rem(me_d + dd + n_dom, n_dom),
        }

    barrier = pltpu.get_barrier_semaphore()
    for step in BLK_STEPS:
        pl.semaphore_signal(barrier, inc=1, device_id=peer(step, 0), device_id_type=MESH)
    for step in OFFSETS:
        pl.semaphore_signal(barrier, inc=1, device_id=peer(0, step), device_id_type=MESH)

    local = []
    for i, (src, dst) in enumerate(
        (
            (pos_hbm, pos_v),
            (lin_hbm, lin_v),
            (bur_hbm, bur_v),
            (mob_hbm, mob_v),
            (clo_hbm, close.at[G0]),
            (map_hbm, maps.at[0]),
        )
    ):
        copy = pltpu.make_async_copy(src, dst, local_sem.at[i])
        copy.start()
        local.append(copy)

    for copy in local[:4]:
        copy.wait()
    state = group.at[G0]
    for first, ref in ((0, pos_v), (24, lin_v), (48, bur_v), (72, mob_v)):
        for k in range(ref.shape[0]):
            for q in range(CELLS):
                state[pl.ds(first + k * 8 + q, 1), :] = ref[pl.ds(k, 1), pl.ds(q * LANES, LANES)]

    pl.semaphore_wait(barrier, len(BLK_STEPS) + len(OFFSETS))

    sends = []

    def send(src, dst, device):
        i = len(sends)
        copy = pltpu.make_async_remote_copy(
            src_ref=src,
            dst_ref=dst,
            send_sem=send_sem.at[i],
            recv_sem=recv_sem.at[i],
            device_id=device,
            device_id_type=MESH,
        )
        copy.start()
        sends.append(copy)
        return copy

    blk_copies = [
        send(state.at[pl.ds(0, 72)], far_blk.at[i], peer(step, 0))
        for i, step in enumerate(BLK_STEPS)
    ]

    def landing(o, outer):
        return 8 + (o < 0) if outer else slot_of(o)

    def halves(ref, components, half):
        view = ref.reshape(ref.shape[0] // 8, 8, LANES)
        return view.at[components, pl.ds(4 * half, 4), :]

    def send_maps(k, outer):
        result = []
        for o in (k, -k):
            cols = pl.ds(256 * ((o > 0) == outer), 256)
            result.append(
                send(map_hbm.at[:, cols], maps.at[1 + landing(o, outer), :, cols], peer(0, -o))
            )
        return result

    def send_statics(k, outer):
        result = []
        for o in (k, -k):
            half = (o > 0) == outer
            result.append(
                send(
                    halves(state, pl.ds(3, 7), half),
                    halves(dom_in.at[landing(o, outer)], pl.ds(3, 7), half),
                    peer(0, -o),
                )
            )
        return result

    def send_first(k):
        pairs = (k, -k)
        return [
            send(state.at[pl.ds(0, ROWS_SETUP)], dom_in.at[slot_of(o)], peer(0, -o)) for o in pairs
        ] + [send(map_hbm, maps.at[1 + slot_of(o)], peer(0, -o)) for o in pairs]

    def send_close(target, k, outer):
        result = []
        for o in (k, -k):
            cols = pl.ds(512 * ((o > 0) == outer), 512)
            result.append(send(clo_hbm.at[:, cols], close.at[target, :, cols], peer(0, -o)))
        return result

    copies_first = send_first(1)
    copies_second = (
        send_close(G1, 1, False)
        + send_statics(2, False)
        + send_maps(2, False)
        + send_statics(3, False)
        + send_maps(3, False)
        + send_close(G2, 2, False)
    )

    own_pos = [state[pl.ds(8 * k, 8), :] for k in range(3)]
    centres = [jnp.mean(rows, axis=1, keepdims=True) for rows in own_pos]
    one = jnp.ones((8, LANES), F32)
    zero = jnp.zeros((8, LANES), F32)

    def put_features(rows_of, target, at):
        pos = [rows_of(k) - centres[k] for k in range(3)]
        line = [rows_of(3 + k) for k in range(3)]
        burg = [rows_of(6 + k) for k in range(3)]
        square = pos[0] * pos[0] + pos[1] * pos[1] + pos[2] * pos[2]
        products = [b * l for b in burg for l in line]
        if target:
            rest = [-2.0 * p for p in pos] + [square, one, zero, zero]
        else:
            rest = pos + [one, square + LONG_CORE * LONG_CORE, zero, zero]
            for k in range(3):
                feat_pos[at, pl.ds(8 * k, 8), :] = pos[k]
        for f, value in enumerate(products + rest):
            for piece, part in enumerate(split3(value)):
                feat[at, pl.ds((piece * 16 + f) * 8, 8), :] = part

    put_features(lambda k: state[pl.ds(8 * k, 8), :], True, 0)
    numerator_row = lax.broadcasted_iota(jnp.int32, (16, LANES), 0) < 9

    def build(q, carry):
        part = [feat[0, pl.ds(piece * 128 + q, 16, stride=8), :] for piece in range(3)]
        for half in range(2):
            keep = numerator_row if half == 0 else jnp.logical_not(numerator_row)
            rows = jnp.concatenate(
                [jnp.where(keep, part[i], 0.0) for i in (0, 0, 1, 0, 1, 2)]
                + [jnp.zeros((32, LANES), F32)],
                axis=0,
            )
            turned = rows.T.astype(BF16)
            for part_at in range(PARTS):
                lhs[q, pl.ds((2 * part_at + half) * PART, PART), :] = turned[
                    part_at * PART : (part_at + 1) * PART
                ]
        return carry

    lax.fori_loop(0, CELLS, build, 0)

    def long_blocks(count, first):
        def cell(q, carry):
            rhs = []
            for s in range(count):
                part = [feat[s, pl.ds(piece * 128 + q, 16, stride=8), :] for piece in range(3)]
                rhs.append(
                    jnp.concatenate(
                        [part[i] for i in (0, 1, 0, 2, 1, 0)] + [jnp.zeros((32, LANES), F32)],
                        axis=0,
                    ).astype(BF16)
                )
            for part_at in range(PARTS):
                rows = pl.ds(part_at * PART, PART)
                total = None if first else [acc[q, k, rows, :] for k in range(4)]
                for s in range(count):
                    both = jnp.dot(
                        lhs[q, pl.ds(2 * part_at * PART, 2 * PART), :],
                        rhs[s],
                        preferred_element_type=F32,
                    )
                    inverse = lax.rsqrt(both[PART:])
                    w = both[:PART] * inverse * (inverse * inverse)
                    terms = [w * feat_pos[s, pl.ds(8 * k + q, 1), :] for k in range(3)] + [w]
                    total = terms if total is None else [a + b for a, b in zip(total, terms)]
                for k in range(4):
                    acc[q, k, rows, :] = total[k]
            return carry

        lax.fori_loop(0, CELLS, cell, 0, unroll=4)

    put_features(lambda k: state[pl.ds(8 * k, 8), :], False, 0)
    long_blocks(1, True)
    row = lax.broadcasted_iota(jnp.int32, (8, LANES), 0)
    low_half = row < 4

    def merge(source, rows, k, outer, first=None):
        first = slot_of(k) if first is None else first
        above, below = source[first, rows, :], source[first + 1, rows, :]
        if outer:
            return jnp.where(low_half, below, above)
        return jnp.where(low_half, above, below)

    near = {G1: (1, False), G2: (2, False), H1: (1, True), G3: (3, False), G4: (4, False), H2: (2, True)}

    def merge_into(target, first, source, source_first, components, groups, slot=None):
        for g in groups:
            k, outer = near[g]
            for c in range(components):
                target[g, pl.ds(first + 8 * c, 8), :] = merge(
                    source, pl.ds(source_first + 8 * c, 8), k, outer, slot
                )

    def put_maps(source, slot, tiles):
        for j in tiles:
            map_all[pl.ds((slot * 4 + j) * SUBS, SUBS), :] = maps[
                source, :, pl.ds(j * LANES, LANES)
            ]

    def put_near_maps(k):
        put_maps(1 + slot_of(k), 1 + slot_of(k), (0, 1))
        put_maps(1 + slot_of(-k), 1 + slot_of(-k), (2, 3))

    def pick_windows(t, n_domains, n_groups, tile_of, target, start=0):
        for domain in DOMAINS[start:n_domains]:
            for g, first, slot, tile, served in windows_of(domain):
                place = map_all[pl.ds((slot * 4 + tile) * SUBS + t, 1), :]
                place = jnp.broadcast_to(place, (8, LANES))
                lane = place & 127
                at = (place >> 7) & 3
                picked = [take_lanes(tile_of(g, first + i), lane) for i in range(4)]
                odd = (at & 1) != 0
                result = jnp.where(
                    at >= 2,
                    jnp.where(odd, picked[3], picked[2]),
                    jnp.where(odd, picked[1], picked[0]),
                )
                for g_to, cell in served:
                    if g_to < n_groups:
                        target[pl.ds((g_to * 8 + cell) * 8, 8), :] = result

    def spread(value):
        return jnp.broadcast_to(value, (8, LANES))

    def close_of(g, s, r):
        return close[g, pl.ds(8 * r, 8), pl.ds(s * LANES, LANES)]

    def dots(mine, other):
        line = mine[0] * other[0] + mine[1] * other[1] + mine[2] * other[2]
        burg = mine[3] * other[3] + mine[4] * other[4] + mine[5] * other[5]
        return line * burg

    def static_rows(g, s):
        return [spread(group[g, pl.ds(24 + 8 * k + s, 1), :]) for k in range(6)]

    def weights_own(g, carry):
        for s in range(CELLS):
            mine = static_rows(g, s)
            for r in range(4):
                index = close_of(g, s, r)
                lane = index & 127
                other = [take_lanes(m, lane) for m in mine]
                weight_own[g, s, pl.ds(8 * r, 8), :] = jnp.where(
                    index < LANES, dots(mine, other), 0.0
                )
        return carry

    def static_tile(g, s):
        return group[g, pl.ds(24 + s, 8, stride=8), :]

    def weights_ghost(t, n_groups, start=0):
        pick_windows(t, DOMAINS_FOR[n_groups], n_groups, static_tile, statics_gh, start)

        def one(g, carry):
            for s in range(CELLS):
                mine = static_rows(g, s)
                base = (g * 8 + s) * 8
                theirs = [spread(statics_gh[pl.ds(base + k, 1), :]) for k in range(6)]
                for r in range(4):
                    index = close_of(g, s, r)
                    lane = index & 127
                    other = [take_lanes(m, lane) for m in theirs]
                    value = jnp.where(index < 2 * LANES, dots(mine, other), 0.0)
                    rows = pl.ds(8 * r, 8)
                    weight[t, g, s, rows, :] = jnp.where(
                        index < LANES, weight_own[g, s, rows, :], value
                    )
            return carry

        lax.fori_loop(start, n_groups, one, 0)

    short_scale = 1.0 / math.sqrt(SLOTS)

    def tiles_in(positions):
        return lambda g, s: positions[g, pl.ds(s, 8, stride=8), :]

    def evaluate(t, n_groups, positions):
        pick_windows(t, DOMAINS_FOR[n_groups], n_groups, tiles_in(positions), ghost)

        def one(g, carry):
            sums = [[], [], []]
            for s in range(CELLS):
                mine = [spread(positions[g, pl.ds(8 * k + s, 1), :]) for k in range(3)]
                base = (g * 8 + s) * 8
                theirs = [spread(ghost[pl.ds(base + k, 1), :]) for k in range(3)]
                total = None
                for r in range(4):
                    index = close_of(g, s, r)
                    lane = index & 127
                    is_ghost = index >= LANES
                    inner = [take_lanes(m, lane) for m in mine]
                    outer = [take_lanes(m, lane) for m in theirs]
                    delta = [
                        m - jnp.where(is_ghost, o, i) for m, o, i in zip(mine, outer, inner)
                    ]
                    radius = (
                        delta[0] * delta[0]
                        + delta[1] * delta[1]
                        + delta[2] * delta[2]
                        + SHORT_CORE * SHORT_CORE
                    )
                    inverse = lax.rsqrt(radius)
                    w = weight[t, g, s, pl.ds(8 * r, 8), :] * inverse * (inverse * inverse)
                    terms = [w * d for d in delta]
                    total = terms if total is None else [a + b for a, b in zip(total, terms)]
                for k in range(3):
                    sums[k].append(total[k])
            for k in range(3):
                frow[g, pl.ds(8 * k, 8), :] = fold_cells(sums[k], row)
            return carry

        lax.fori_loop(0, n_groups, one, 0, unroll=n_groups)

    def drift(g, k):
        rows = pl.ds(8 * k, 8)
        force = group[g, pl.ds(ROW_F + 8 * k, 8), :] + frow[g, rows, :] * short_scale
        return group[g, pl.ds(ROW_MOB, 8), :] * force

    def make_guess(n_groups):
        for g in range(n_groups):
            for k in range(3):
                rows = pl.ds(8 * k, 8)
                first = drift(g, k)
                position = xnow[g, rows, :]
                vfirst[g, rows, :] = first
                xguess[g, rows, :] = position + STEP * first
                xhalf[g, rows, :] = position + (0.5 * STEP) * first

    def advance(n_groups):
        for g in range(n_groups):
            for k in range(3):
                rows = pl.ds(8 * k, 8)
                xnow[g, rows, :] = xhalf[g, rows, :] + (0.5 * STEP) * drift(g, k)

    for copy in local[4:]:
        copy.wait()
    lax.fori_loop(0, 1, weights_own, 0)
    put_maps(0, 0, range(4))
    for i in range(4):
        blk_copies[i].wait_recv()
        put_features(lambda k: far_blk[i, pl.ds(8 * k, 8), :], False, i)
    long_blocks(4, False)

    lane_id = lax.broadcasted_iota(jnp.int32, (LANES, LANES), 1)

    def reduce_cell(q, columns):
        for k in range(4):
            total = jnp.sum(acc[q, k], axis=1, keepdims=True)
            columns = jnp.where(lane_id == k * 8 + q, total, columns)
        return columns

    columns = lax.fori_loop(
        0, CELLS, reduce_cell, jnp.zeros((LANES, LANES), F32), unroll=8
    )
    sums = columns.T
    scale = 1.0 / math.sqrt(5 * LANES)
    for k in range(3):
        force = ((own_pos[k] - centres[k]) * sums[24:32] - sums[8 * k : 8 * k + 8]) * scale
        state[pl.ds(ROW_F + 8 * k, 8), :] = force


    for copy in copies_first:
        copy.wait_recv()
    merge_into(group, 0, dom_in, 0, 10, (G1, H1))
    put_maps(1, 1, range(4))
    put_maps(2, 2, range(4))
    xnow[G0, pl.ds(0, 24), :] = state[pl.ds(0, 24), :]
    xnow[G1, pl.ds(0, 24), :] = group[G1, pl.ds(0, 24), :]
    weights_ghost(0, 1)
    evaluate(0, 1, xnow)
    make_guess(1)
    for k in range(3):
        for part, ref in ((0, xguess), (48, xhalf)):
            msend[pl.ds(part + 8 * k, 8), :] = ref[G0, pl.ds(8 * k, 8), :]
        msend[pl.ds(24 + 8 * k, 8), :] = group[G0, pl.ds(ROW_F + 8 * k, 8), :]
    m_copies = []
    for k, count in ((3, 6), (2, 9)):
        for o in (k, -k):
            part = functools.partial(halves, components=pl.ds(0, count), half=o < 0)
            m_copies.append(send(part(msend), part(mrecv.at[slot_of(o)]), peer(0, -o)))
    m_copies += [send(msend, mrecv.at[slot_of(o)], peer(0, -o)) for o in OFFSETS[:2]]
    copies_third = (
        send_close(H1, 1, True)
        + send_close(G3, 3, False)
        + send_statics(2, True)
        + send_maps(2, True)
        + send_statics(4, False)
        + send_maps(4, False)
    )

    for copy in copies_second:
        copy.wait_recv()
    merge_into(group, 24, dom_in, 24, 7, (G2, G3))
    put_near_maps(2)
    put_near_maps(3)
    lax.fori_loop(1, 3, weights_own, 0)
    weights_ghost(0, 3, 1)
    weights_ghost(1, 2)
    for copy in m_copies:
        copy.wait_recv()
    merge_into(xguess, 0, mrecv, 0, 3, (G1, G2, H1, G3))
    merge_into(xhalf, 0, mrecv, 48, 3, (G1, G2))
    merge_into(group, ROW_F, mrecv, 24, 3, (G1, G2, H1, G3))
    evaluate(0, 3, xguess)
    advance(3)
    evaluate(1, 2, xnow)
    make_guess(2)
    evaluate(1, 1, xguess)
    advance(1)
    xsend[...] = xnow[G0, pl.ds(0, 24), :]
    x_copies = [send(xsend, xrecv.at[slot_of(o)], peer(0, -o)) for o in OFFSETS[:4]]
    for o in OFFSETS[4:]:
        part = functools.partial(halves, components=pl.ds(0, 3), half=o < 0)
        x_copies.append(send(part(xsend), part(xrecv.at[slot_of(o)]), peer(0, -o)))

    for copy in copies_third:
        copy.wait_recv()
    merge_into(group, 24, dom_in, 24, 7, (G4,))
    merge_into(group, 24, dom_in, 24, 7, (H2,), 8)
    put_near_maps(4)
    put_maps(9, 3, (2, 3))
    put_maps(10, 4, (0, 1))
    lax.fori_loop(3, 5, weights_own, 0)
    weights_ghost(2, 5)
    weights_ghost(3, 2)
    for copy in x_copies:
        copy.wait_recv()
    merge_into(xnow, 0, xrecv, 0, 3, (G1, G2, H1, G3, G4, H2))
    evaluate(2, 5, xnow)
    make_guess(5)
    evaluate(2, 3, xguess)
    advance(3)
    evaluate(3, 2, xnow)
    make_guess(2)
    evaluate(3, 1, xguess)
    for k in range(3):
        twice = vfirst[G0, pl.ds(8 * k, 8), :] + drift(G0, k)
        position = xnow[G0, pl.ds(8 * k, 8), :]
        for q in range(CELLS):
            cols = pl.ds(q * LANES, LANES)
            pos_out[pl.ds(k, 1), cols] = position[q : q + 1, :]
            vel_out[pl.ds(k, 1), cols] = twice[q : q + 1, :]

    for copy in sends:
        copy.wait_send()


def solution(mesh):
    n_blk, n_dom = mesh.shape["blk"], mesh.shape["dom"]

    def step(positions, line_vectors, burgers, mobility, close_list, ghost_map):
        count = positions.shape[1]
        anywhere = pl.BlockSpec(memory_space=pl.ANY)
        vmem = pl.BlockSpec(memory_space=pltpu.VMEM)
        shape = jax.ShapeDtypeStruct((3, count), F32)
        n_sends = 4 + 4 + 12 + 12 + 6 + 8
        base, twice = pl.pallas_call(
            functools.partial(kernel, n_blk, n_dom),
            out_shape=(shape, shape),
            in_specs=[anywhere] * 6,
            out_specs=(vmem, vmem),
            scratch_shapes=[
                pltpu.VMEM((3, count), F32),
                pltpu.VMEM((3, count), F32),
                pltpu.VMEM((3, count), F32),
                pltpu.VMEM((1, count), F32),
                pltpu.VMEM((4, 72, LANES), F32),
                pltpu.VMEM((10, ROWS_SETUP, LANES), F32),
                pltpu.VMEM((7, ROWS_ALL, LANES), F32),
                pltpu.VMEM((5, SLOTS, count), jnp.int32),
                pltpu.VMEM((11, SUBS, 512), jnp.int32),
                pltpu.VMEM((144, LANES), jnp.int32),
                pltpu.VMEM((4, 384, LANES), F32),
                pltpu.VMEM((4, 24, LANES), F32),
                pltpu.VMEM((CELLS, 256, LANES), BF16),
                pltpu.VMEM((CELLS, 4, LANES, LANES), F32),
                pltpu.VMEM((320, LANES), F32),
                pltpu.VMEM((5, CELLS, SLOTS, LANES), F32),
                pltpu.VMEM((SUBS, 5, CELLS, SLOTS, LANES), F32),
                pltpu.VMEM((320, LANES), F32),
                pltpu.VMEM((5, 24, LANES), F32),
                pltpu.VMEM((5, 24, LANES), F32),
                pltpu.VMEM((7, 64, LANES), F32),
                pltpu.VMEM((5, 64, LANES), F32),
                pltpu.VMEM((5, 24, LANES), F32),
                pltpu.VMEM((72, LANES), F32),
                pltpu.VMEM((6, 72, LANES), F32),
                pltpu.VMEM((24, LANES), F32),
                pltpu.VMEM((8, 24, LANES), F32),
                pltpu.SemaphoreType.DMA((6,)),
                pltpu.SemaphoreType.DMA((n_sends,)),
                pltpu.SemaphoreType.DMA((n_sends,)),
            ],
            compiler_params=pltpu.CompilerParams(collective_id=0, has_side_effects=True),
        )(positions, line_vectors, burgers, mobility.reshape(1, count), close_list, ghost_map)
        return base + (0.5 * STEP) * twice, 0.5 * twice

    both = ("blk", "dom")
    return jax.shard_map(
        step,
        mesh=mesh,
        in_specs=(
            P(None, both),
            P(None, both),
            P(None, both),
            P(both),
            P(None, both),
            P(None, both),
        ),
        out_specs=(P(None, both), P(None, both)),
        check_vma=False,
    )
```
